32 devices in a mesh: grp: 4 (over x, core), blk: 8 (over z, y).
Axes of the slice: x: 2, y: 2, z: 4, core: 2. Of those that a mesh axis runs over, the one named last changes fastest.
Arguments:
- pair_density: bfloat16 [2048, 8192], P('grp', 'blk'), may hold values from -14 to 14
- energies: float32 [2048], P('grp'), may hold values from 1 to 4
- batch_live: int32 [4], replicated, may hold values from 1 to 512, 1280 in all
- coulomb_root: float32 [8192], replicated, may hold values from 0.5 to 2
Outputs:
- polarized: bfloat16 [4, 8192, 8192], P('grp', 'blk')
- screened: float32 [4, 8192, 128], P('grp', 'blk')
The draws below stay inside these ranges and needn't reach their ends.
Inputs may be any that keep to these rules, and one draw needn't show every extreme that they name: Group g's live transitions are its first batch_live[g] slots of 512; at least one group is full.
All inputs are finite; a program needn't handle non-finite values.
Results may differ from the reference program's by a relative error of at most 0.03.
Values may be sent and summed in bfloat16 or wider, within the bound.
A program may use at most 128 MiB of HBM per device.

```python
import math
import jax
import jax.numpy as jnp
import numpy as np

G = 8192
T_GRP = 512
CW = 128
DYSON = 2
TRANS = 2048
GROUPS = 4


def steps_of(own_key, extent, cuts, smallest, largest):
    gain, own = 1.0, jax.random.fold_in(own_key, 6)
    for position, parts in cuts:
        heights = jnp.exp(jax.random.uniform(jax.random.fold_in(own, position), (parts,), jnp.float32, smallest / len(cuts), largest / len(cuts)))
        gain = gain * jnp.repeat(heights, extent[position] // parts).reshape([-1 if axis == position else 1 for axis in range(len(extent))])
    return gain


def split_up(count, total, bound, skew):
    weights = [(1 << 20) // math.isqrt(rank ** skew) + 1 for rank in range(2, count + 1)]
    spare, counts = total - bound - (count - 1), [1] * (count - 1)
    while spare > 0:
        free = [i for i in range(count - 1) if counts[i] < bound]
        mass, budget = sum([weights[i] for i in free]), spare
        for i in free:
            more = min(bound - counts[i], max(1, budget * weights[i] // mass), spare)
            counts[i] = counts[i] + more
            spare = spare - more
    return np.array([bound] + counts)


def uneven(rng, amount, total, most, slope):
    if amount == 2:
        one = jax.random.randint(rng, (), max(1, total - most), min(most, total - 1) + 1)
        return jnp.stack([one, total - one])
    sizes = jnp.asarray(split_up(amount, total, most, slope), jnp.int32)
    pairs = (amount - 1) // 2
    giver, taker = sizes[1:1 + 2 * pairs:2], sizes[2:2 + 2 * pairs:2]
    room = jnp.minimum(giver - 1, most - taker)
    passed = jax.random.randint(jax.random.fold_in(rng, 1), (pairs,), 0, 1 << 20) % (room + 1)
    sizes = sizes.at[1:1 + 2 * pairs:2].set(giver - passed).at[2:2 + 2 * pairs:2].set(taker + passed)
    return sizes[jax.random.permutation(jax.random.fold_in(rng, 2), amount)]


def gaussian(stream_key, dims, deviation, most, pieces=(), held_as=jnp.bfloat16):
    array = jax.random.normal(stream_key, dims, jnp.float32) * deviation
    if len(pieces) > 0:
        array = steps_of(stream_key, dims, pieces, -0.22, 0.18) * array
    return jnp.clip(array, min=-most, max=most).astype(held_as)


def setup_inputs(seed: int = 0) -> dict:
    seeds = jax.random.split(jax.random.key(seed), 5)
    pair_density = gaussian(seeds[0], (TRANS, G), 3.0, 14.0, ((0, 4), (1, 8)))
    energies = jnp.clip(jnp.exp(math.log(4.0) - 1.3862944 * jax.random.uniform(seeds[1], (TRANS,), jnp.float32) ** steps_of(seeds[1], (TRANS,), ((0, 4),), -0.2, 0.2)), 1.0, 4.0)
    batch_live = uneven(seeds[2], GROUPS, 5 * T_GRP // 2, T_GRP, 2).astype(jnp.int32)
    coulomb_root = jnp.clip(jnp.exp(jax.random.uniform(seeds[3], (G,), jnp.float32, math.log(0.5), math.log(2.0))), 0.5, 2.0)
    return dict(pair_density=pair_density, energies=energies, batch_live=batch_live, coulomb_root=coulomb_root)


def reference(pair_density, energies, batch_live, coulomb_root):
    positions = jnp.arange(TRANS, dtype=jnp.int32)
    limits = batch_live[positions // T_GRP]
    is_live = (positions % T_GRP < limits).astype(jnp.float32)
    norm_factor = 1.0 / math.sqrt(TRANS)
    dense = pair_density.astype(jnp.float32)
    polar_list = []
    screen_list = []
    for freq_index in range(GROUPS):
        frequency = 0.6 * freq_index
        weight = -2.0 * energies / (energies * energies + frequency * frequency) * is_live * norm_factor
        scaled = (weight[:, None] * dense).astype(jnp.bfloat16)
        chi = jnp.dot(scaled.T, pair_density, preferred_element_type=jnp.float32)
        tiles = coulomb_root[:, None] * chi * coulomb_root[None, :]
        polarized = tiles.astype(jnp.bfloat16)
        window = tiles[:, :CW]
        state = window
        for dyson_step in range(DYSON):
            product = jnp.dot(polarized, state.astype(jnp.bfloat16), preferred_element_type=jnp.float32)
            state = window + 8.0 / G * product
        polar_list.append(polarized)
        screen_list.append(state)
    return (jnp.stack(polar_list), jnp.stack(screen_list))
```

```python
import functools
import math

import jax
import jax.numpy as jnp
from jax import lax
from jax.experimental import pallas as pl
from jax.experimental.pallas import tpu as pltpu
from jax.sharding import PartitionSpec as P

G = 8192
CW = 128
DYSON = 2
LANES = 128
MESH = pl.DeviceIdType.MESH
VMEM_LIMIT = 34 * 1024 * 1024
FINISH_LIMIT = 30 * 1024 * 1024
OWN, XO, YO, YD, ZN, XN, YN, ZD, RD = range(9)
RELAY_Y = (3,)
EVENTS = (
    0, 1, 2, 3, 16, 17, 18, 19, 32, 33, 34, 35, 48, 49, 50, 51, 68, 69, 70, 71, 72, 73, 74,
    75, 76, 77, 78, 79, 84, 85, 86, 87, 88, 89, 90, 91, 92, 93, 94, 95, 100, 101, 102, 103,
    104, 105, 106, 107, 108, 109, 110, 111, 116, 117, 118, 120, 121, 122, 124, 125, 126, 135,
    139, 143,
)
PLANS = (
    (
        (
            0, 69, 2, 3, 71, 18, 1, 50, 32, 16, 68, 76, 70, 73, 19, 17, 85, 87, 84, 34, 75,
        ),
        (
            1, 0, 5, 2, 4, 12, 3, 8, 13, 9, 11, 7, 15, 10, 14, 6,
        ),
        (
            (108, 92, 48), (), (), (101, 72), (), (33, 35, 105, 78, 86, 74), (89,), (), (49,
            117, 100, 102), (77, 94, 51), (), (116,), (79, 90, 88, 126), (104,), (107, 91), (93,
            103, 95), (), (), (109, 118, 139), (110, 121), (122,), (135,), (), (106, 143, 125,
            111), (120,), (), (), (124,), (), (), (), (),
        ),
        (),
    ),
    (
        (
            1, 0, 2, 17, 3, 70, 68, 74, 73, 75, 16, 76, 84, 72, 86, 49, 18, 34, 32, 78, 100, 19,
            71,
        ),
        (
            0, 4, 1, 6, 8, 12, 5, 2, 14, 9, 3, 10, 13, 15, 7, 11,
        ),
        (
            (), (69, 107, 118, 90), (), (48, 102, 116, 91, 77), (79,), (105,), (89,), (120, 88),
            (106,), (126, 33, 92), (110, 35, 94, 87, 121, 50, 124), (108, 85), (), (), (), (122,
            117, 103), (104, 51), (), (95, 125), (), (), (101, 93), (), (143, 109), (111, 135),
            (), (), (), (), (139,), (), (),
        ),
        (),
    ),
)


def live_weights(all_energy, batch_live, slots, total_slots, group_ids, frequencies, norm_factor):
    positions = jnp.arange(total_slots, dtype=jnp.int32)
    owner_match = (positions // slots)[:, None] == group_ids[None, :]
    limits = jnp.sum(jnp.where(owner_match, batch_live[None, :], 0), axis=1)
    is_live = (positions % slots < limits).astype(jnp.float32)
    weight = (
        -2.0
        * all_energy[None, :]
        / (all_energy[None, :] * all_energy[None, :] + frequencies[:, None] * frequencies[:, None])
    )
    return weight * is_live[None, :] * norm_factor


def plain_body(pair_density, energies, batch_live, coulomb_root):
    slots = pair_density.shape[0]
    width_own = pair_density.shape[1]
    group_count = lax.axis_size("grp")
    block_count = lax.axis_size("blk")
    total_slots = slots * group_count
    group_index = lax.axis_index("grp")
    block_index = lax.axis_index("blk")
    norm_factor = 1.0 / math.sqrt(total_slots)
    own_root = lax.dynamic_slice_in_dim(coulomb_root, block_index * width_own, width_own)
    group_ids = jnp.arange(group_count, dtype=jnp.int32)
    row_density, all_energy = (
        lax.all_gather(pair_density, "grp", axis=0, tiled=True),
        lax.all_gather(energies.astype(jnp.bfloat16), "grp", axis=0, tiled=True).astype(
            energies.dtype
        ),
    )
    frequencies = 0.6 * jnp.arange(group_count, dtype=jnp.float32)
    weight = live_weights(
        all_energy, batch_live, slots, total_slots, group_ids, frequencies, norm_factor
    )
    scaled = (weight[:, :, None] * row_density.astype(jnp.float32)[None, :, :]).astype(jnp.bfloat16)
    sub_width = width_own // group_count
    my_slice = lax.dynamic_slice_in_dim(row_density, group_index * sub_width, sub_width, 1)
    root_table = jnp.reshape(coulomb_root, (block_count, group_count, sub_width))
    my_roots = jnp.reshape(
        lax.dynamic_index_in_dim(root_table, group_index, 1, keepdims=False), (-1,)
    )
    chi = jnp.einsum(
        "ftc,tk->fck",
        scaled,
        lax.all_gather(my_slice, "blk", axis=1, tiled=True),
        preferred_element_type=jnp.float32,
    )
    quarter = own_root[None, :, None] * chi * my_roots[None, None, :]
    received = lax.all_to_all(
        quarter.astype(jnp.bfloat16), "grp", split_axis=0, concat_axis=0, tiled=True
    )
    received = jnp.reshape(received, (group_count, width_own, block_count, sub_width))
    polarized = jnp.reshape(
        jnp.transpose(received, (1, 2, 0, 3)), (width_own, width_own * block_count)
    )
    lead_blocks = (CW + width_own - 1) // width_own
    lead = quarter[:, :, : lead_blocks * sub_width]
    lead_back = lax.all_to_all(
        lead.astype(jnp.bfloat16), "grp", split_axis=0, concat_axis=0, tiled=True
    ).astype(lead.dtype)
    lead_back = jnp.reshape(lead_back, (group_count, width_own, lead_blocks, sub_width))
    window = jnp.reshape(
        jnp.transpose(lead_back, (1, 2, 0, 3)), (width_own, lead_blocks * width_own)
    )[:, :CW]
    state = window
    for dyson_step in range(DYSON):
        rounded = state.astype(jnp.bfloat16)
        product = jnp.dot(
            polarized,
            lax.all_gather(rounded, "blk", axis=0, tiled=True),
            preferred_element_type=jnp.float32,
        )
        state = window + 8.0 / G * product
    return (polarized[None], state[None])


def far_plane(z, nz, k):
    edge = jnp.minimum(z, nz - 1 - z)
    low = k if k > 1 else jnp.where(edge == 0, k, 1 - k)
    return jnp.where(2 * z < nz, low, nz - 1 - low)


def stream_kernel(
    rows_ref, energy_ref, live_ref, root_ref,
    out_ref, at_ref, m_ref, w_ref, lead_ref,
    p_ref, raw_ref, surplus_ref, spare_ref, energies_ref, column_ref, source_ref, scaled_ref,
    pick_a, pick_b, pick_s, stage_ref,
    recv, s_x, s_y, s_z, s_pair, s_local, s_raw, r_raw, s_sur, r_sur, s_energy, r_energy, s_out,
):
    g, b = lax.axis_index("grp"), lax.axis_index("blk")
    x, c = g // 2, g % 2
    z, y = b // 2, b % 2
    nz = p_ref.shape[0] // 2
    slots, width = rows_ref.shape
    packed, half = p_ref.shape[2], p_ref.shape[3]
    share, core = packed // 2, packed // 4
    first = (packed - 2 * slots) // 2
    second = core - first
    edge = jnp.minimum(z, nz - 1 - z)
    to_x = ((1 - x) * 2 + c, b)
    to_y = (g, z * 2 + 1 - y)
    to_pair = (x * 2 + 1 - c, b)
    inward = jnp.where(2 * z < nz, z + 1, z - 1)
    outward = 2 * z - inward
    to_in = (g, inward * 2 + y)
    to_out = (g, outward * 2 + y)
    middle = edge == 1

    barrier = pltpu.get_barrier_semaphore()

    def greet(to):
        pl.semaphore_signal(barrier, inc=1, device_id=to, device_id_type=MESH)

    keep_rows = [
        pltpu.make_async_copy(
            rows_ref.at[:, h * half:(h + 1) * half],
            raw_ref.at[c, :, h * half:(h + 1) * half], s_local.at[h])
        for h in range(2)
    ]
    keep_energy = pltpu.make_async_copy(energy_ref.at[0], energies_ref.at[g], s_local.at[2])
    for copy in keep_rows:
        copy.start()
    keep_energy.start()
    for to in (to_x, to_y, to_pair, to_in):
        greet(to)
    pl.when(middle)(lambda: greet(to_out))
    pl.semaphore_wait(barrier, 4 + middle.astype(jnp.int32))

    def rows_pair(h, who):
        return pltpu.make_async_remote_copy(
            src_ref=rows_ref.at[:, h * half:(h + 1) * half],
            dst_ref=raw_ref.at[who, :, h * half:(h + 1) * half],
            send_sem=s_raw.at[h], recv_sem=r_raw.at[h], device_id=to_pair, device_id_type=MESH)

    def energy_to(way, to, who):
        return pltpu.make_async_remote_copy(
            src_ref=energies_ref.at[who] if way == 2 else energy_ref.at[0],
            dst_ref=energies_ref.at[who], send_sem=s_energy.at[way], recv_sem=r_energy.at[who],
            device_id=to, device_id_type=MESH)

    g_x, g_pair, g_far = (1 - x) * 2 + c, x * 2 + 1 - c, (1 - x) * 2 + 1 - c
    for h in range(2):
        rows_pair(h, c).start()
    energy_to(0, to_x, g).start()
    energy_to(1, to_pair, g).start()

    live0, live1 = live_ref[2 * x], live_ref[2 * x + 1]
    count = live0 + live1

    def one_hot(ref, source):
        at = lax.broadcasted_iota(jnp.int32, ref.shape, 1)
        ref[...] = (source == at).astype(jnp.float32).astype(jnp.bfloat16)

    def column_iota(size):
        return lax.broadcasted_iota(jnp.int32, (size, 1), 0)

    position = column_iota(pick_s.shape[0]) + (share + c * pick_s.shape[0])
    one_hot(pick_s, jnp.where(position < count, position - live0, -1))
    slot = column_iota(first) + c * first
    one_hot(pick_a, jnp.where(slot < live0, slot, slots + slot - live0))
    slot = column_iota(second) + (2 * first + c * second)
    one_hot(pick_b, jnp.where(
        slot < live0, slot,
        jnp.where(slot < count, slots + slot - live0, 2 * slots + slot - count)))

    def item(ox, ob, cc, kind, h):
        start = ox * share + cc * core + (first if kind else 0)
        size = second if kind else first
        return p_ref.at[ob, h, pl.ds(pl.multiple_of(start, 64), size)]

    def send(ox, ob, p, sem, to, cc=None, h=None):
        cc = c if cc is None else cc
        kind, h = (p // 2, p % 2) if h is None else (p, h)
        ref = item(ox, ob, cc, kind, h)
        return pltpu.make_async_remote_copy(
            src_ref=ref, dst_ref=ref, send_sem=sem, recv_sem=recv.at[ox, ob, cc, kind * 2 + h],
            device_id=to, device_id_type=MESH)

    def over_x(ox, ob, p):
        return send(ox, ob, p, s_x.at[ob, p], to_x)

    def over_y(ox, ob, p):
        return send(ox, ob, p, s_y.at[ox, ob // 2, p], to_y)

    def over_in(ox, ob, p):
        return send(ox, ob, p, s_z.at[0, ox, ob // 2, p], to_in)

    def over_out(ox, ob, p):
        return send(ox, ob, p, s_z.at[1, ox, ob // 2, p], to_out)

    def onward(ox, zz, ob, p):
        low = zz < z
        to = (g, jnp.where(low, z + 1, z - 1) * 2 + y)
        way = jnp.where(low == (2 * z < nz), 0, 1)
        return send(ox, ob, p, s_z.at[way, ox, zz, p], to)

    def over_pair(ox, ob, p):
        return send(ox, ob, p, s_pair.at[ox, ob, p], to_pair)

    def surplus_x(h):
        return pltpu.make_async_remote_copy(
            src_ref=spare_ref.at[h], dst_ref=surplus_ref.at[h, c], send_sem=s_sur.at[0, h],
            recv_sem=r_sur.at[h, c], device_id=to_x, device_id_type=MESH)

    def surplus_pair(h, who):
        return pltpu.make_async_remote_copy(
            src_ref=surplus_ref.at[h, who], dst_ref=surplus_ref.at[h, who],
            send_sem=s_sur.at[1, h], recv_sem=r_sur.at[h, who], device_id=to_pair,
            device_id_type=MESH)

    def dot(left, right):
        return jnp.dot(left, right, preferred_element_type=jnp.float32)

    def raw(who, h):
        return raw_ref[who, :, h * half:(h + 1) * half]

    def fill(kind, h, value):
        start = pl.multiple_of(x * share + c * core + (first if kind else 0), 64)
        p_ref[b, h, pl.ds(start, second if kind else first)] = value.astype(jnp.bfloat16)

    for h in range(2):
        keep_rows[h].wait()
        rows_pair(h, 1 - c).wait_recv()
        spare_ref[h] = dot(pick_s[...], raw(1, h)).astype(jnp.bfloat16)
        surplus_x(h).start()
    for h in range(2):
        fill(0, h, dot(pick_a[:, :slots], raw(0, h)) + dot(pick_a[:, slots:], raw(1, h)))

    def prepare(h):
        surplus_x(h).wait_recv()
        surplus_pair(h, c).start()
        value = dot(pick_b[:, :slots], raw(0, h)) + dot(pick_b[:, slots:2 * slots], raw(1, h))
        surplus_pair(h, 1 - c).wait_recv()
        tail = pick_b.shape[1] - 2 * slots
        value += dot(pick_b[:, 2 * slots:2 * slots + tail // 2], surplus_ref[h, 0])
        fill(1, h, value + dot(pick_b[:, 2 * slots + tail // 2:], surplus_ref[h, 1]))

    def event(code):
        t, k, p = code // 16, code // 4 % 4, code % 4
        zz = far_plane(z, nz, k) if k else z
        ox = x if t in (OWN, YO, ZN, YN) else 1 - x
        ob = zz * 2 + (y if t in (OWN, XO, ZN, XN) else 1 - y)
        if t == OWN:
            if p >= 2:
                prepare(p % 2)
        else:
            send(ox, ob, p, s_pair.at[ox, ob, p], to_pair).wait_recv()
        return moves(t, k, p, zz, ox, ob, "start")

    def moves(t, k, p, zz, ox, ob, act):
        def do(make):
            getattr(make(), act)()

        if t in (OWN, ZN):
            if t == ZN:
                pl.when(middle)(lambda: do(lambda: onward(ox, zz, ob, p)))
            else:
                do(lambda: over_in(ox, ob, p))
                pl.when(middle)(lambda: do(lambda: over_out(ox, ob, p)))
            do(lambda: over_y(ox, ob, p))
            do(lambda: over_x(ox, ob, p))
        elif t == ZD:
            pl.when(middle)(lambda: do(lambda: onward(ox, zz, ob, p)))
        elif t == XO:
            do(lambda: over_y(ox, ob, p))
        elif t == YD and p < 3:
            do(lambda: over_in(ox, ob, p))
            pl.when(middle)(lambda: do(lambda: over_out(ox, ob, p)))
        elif t == XN and p == 3 and k in RELAY_Y:
            do(lambda: over_y(ox, ob, p))
        elif t == YN and p == 3 and k not in RELAY_Y:
            do(lambda: over_x(ox, ob, p))
        do(lambda: over_pair(ox, ob, p))

    def run(plans):
        for kind, codes in enumerate(plans):
            if codes:
                @pl.when(edge == kind)
                def _():
                    for code in codes:
                        event(code)

    def weights():
        energy_to(0, to_x, g_x).wait_recv()
        energy_to(2, to_pair, g_x).start()
        keep_energy.wait()
        energy_to(1, to_pair, g_pair).wait_recv()
        energy_to(2, to_pair, g_far).wait_recv()
        for k in range(4):
            column_ref[k * slots:(k + 1) * slots] = jnp.broadcast_to(
                energies_ref[k], (LANES, slots)).T
        row = lax.broadcasted_iota(jnp.int32, (1, packed), 1)
        upper = row >= share
        row = row - jnp.where(upper, share, 0)
        other = row >= core
        row = row - jnp.where(other, core, 0)
        late = row >= first
        row = row + jnp.where(
            late, 2 * first - first + jnp.where(other, second, 0), jnp.where(other, first, 0))
        a0, a1, a2, a3 = (live_ref[k] for k in range(4))
        n0 = jnp.where(upper, a2, a0)
        n1 = n0 + jnp.where(upper, a3, a1)
        base = jnp.where(upper, 2 * slots, 0)
        across = jnp.where(upper, slots - a0, 3 * slots - a2) + share
        source_ref[...] = jnp.where(
            row < n0, base + row,
            jnp.where(row < n1, base + slots + row - n0, across + row - n1))

        @pl.loop(0, packed // LANES)
        def _(k):
            part = pl.ds(pl.multiple_of(k * LANES, LANES), LANES)
            hit = source_ref[:, part] == lax.broadcasted_iota(
                jnp.int32, (4 * slots, LANES), 0)
            w_ref[:, part] = jnp.sum(
                jnp.where(hit, column_ref[...], 0.0), axis=0, keepdims=True)

        energy = w_ref[...]
        frequency = 0.6 * g.astype(jnp.float32)
        w_ref[...] = -2.0 * energy / (energy * energy + frequency * frequency) * (
            1.0 / math.sqrt(4 * slots))

    m_ref[...] = jnp.zeros_like(m_ref)
    leading = [plan[0] for plan in PLANS]
    early = [codes[:2] for codes in leading]
    run(early)
    weights()
    run([codes[2:] for codes in leading])

    def from_pair(ox, ob, kind, h):
        send(ox, ob, kind, s_pair.at[ox, ob, kind * 2 + h], to_pair, cc=1 - c, h=h).wait_recv()

    def ready(ob, h):
        for ox in range(2):
            for kind in range(2):
                from_pair(ox, ob, kind, h)

    for h in range(2):
        ready(b, h)
        for k in range(2):
            part = slice(k * half // 2, (k + 1) * half // 2)
            start = pl.multiple_of(b * width + h * half + k * (half // 2), half // 2)
            own = p_ref[b, h, :, part].astype(jnp.float32) * root_ref[:, pl.ds(start, half // 2)]
            rows = slice(h * half + part.start, h * half + part.stop)
            at_ref[rows] = (own.T * w_ref[...]).astype(jnp.bfloat16)

    units = 4 * nz

    def put(ob, h, lane):
        return pltpu.make_async_copy(stage_ref.at[lane], out_ref.at[ob, h], s_out.at[lane])

    @pl.loop(0, units)
    def _(step):
        def pick(table):
            value = table[0]
            for k in range(1, units):
                value = jnp.where(step == k, table[k], value)
            return value

        unit = jnp.where(edge == 0, pick(PLANS[0][1]), pick(PLANS[1][1]))
        k, other, h = unit // 4, unit // 2 % 2, unit % 2
        zz = z
        for j in range(1, nz):
            zz = jnp.where(k == j, far_plane(z, nz, j), zz)
        ob = zz * 2 + jnp.where(other == 1, 1 - y, y)
        root = root_ref[:, pl.ds(pl.multiple_of(ob * width + h * half, half), half)]

        def slot_events(which):
            for s in range(units):
                codes = [plan[2][2 * s + which] for plan in PLANS]
                if any(codes):
                    @pl.when(step == s)
                    def _():
                        run(codes)

        slot_events(0)

        @pl.when(unit >= 2)
        def _():
            ready(ob, h)

        lane = step % 2

        @pl.when(step >= 2)
        def _():
            put(ob, h, lane).wait()

        stage_ref[lane] = (dot(at_ref[...], p_ref[ob, h]) * root).astype(jnp.bfloat16)
        put(ob, h, lane).start()
        slot_events(1)
        scaled_ref[...] = (p_ref[ob, h].astype(jnp.float32) * (root * root)).astype(jnp.bfloat16)
        for a in range(0, packed, 256):
            m_ref[a:a + 256, a:] += lax.dot_general(
                scaled_ref[a:a + 256], p_ref[ob, h, a:], (((1,), (1,)), ((), ())),
                preferred_element_type=jnp.float32)

    run([plan[3] for plan in PLANS])
    lead_ref[...] = p_ref[0, 0, :, :CW]
    for lane in range(2):
        put(b, 0, lane).wait()

    energy_to(0, to_x, g).wait_send()
    energy_to(1, to_pair, g).wait_send()
    energy_to(2, to_pair, g_x).wait_send()
    for h in range(2):
        rows_pair(h, c).wait_send()
        surplus_x(h).wait_send()
        surplus_pair(h, c).wait_send()
    for code in EVENTS:
        t, k, p = code // 16, code // 4 % 4, code % 4
        zz = far_plane(z, nz, k) if k else z
        ox = x if t in (OWN, YO, ZN, YN) else 1 - x
        ob = zz * 2 + (y if t in (OWN, XO, ZN, XN) else 1 - y)
        moves(t, k, p, zz, ox, ob, "wait_send")


def stream(pair_density, energies, batch_live, coulomb_root, blocks):
    slots, width = pair_density.shape
    packed = slots * 5 // 2
    half = width // 2
    first = (packed - 2 * slots) // 2
    second = packed // 4 - first
    spare = (2 * slots - packed // 2) // 2
    nz = blocks // 2
    dma = pltpu.SemaphoreType.DMA
    vmem = pl.BlockSpec(memory_space=pltpu.VMEM)
    bf16, f32 = jnp.bfloat16, jnp.float32
    shape = jax.ShapeDtypeStruct
    return pl.pallas_call(
        stream_kernel,
        out_shape=(
            shape((blocks, 2, width, half), bf16),
            shape((width, packed), bf16),
            shape((packed, packed), f32),
            shape((1, packed), f32),
            shape((packed, CW), bf16),
        ),
        in_specs=[
            pl.BlockSpec(memory_space=pl.ANY), vmem,
            pl.BlockSpec(memory_space=pltpu.SMEM), vmem,
        ],
        out_specs=(pl.BlockSpec(memory_space=pl.ANY),) + (vmem,) * 4,
        scratch_shapes=[
            pltpu.VMEM((blocks, 2, packed, half), bf16),
            pltpu.VMEM((2, slots, width), bf16),
            pltpu.VMEM((2, 2, spare, half), bf16),
            pltpu.VMEM((2, spare, half), bf16),
            pltpu.VMEM((4, 1, slots), f32),
            pltpu.VMEM((4 * slots, LANES), f32),
            pltpu.VMEM((1, packed), jnp.int32),
            pltpu.VMEM((packed, half), bf16),
            pltpu.VMEM((first, 2 * slots), bf16),
            pltpu.VMEM((second, 2 * slots + 2 * spare), bf16),
            pltpu.VMEM((spare, slots), bf16),
            pltpu.VMEM((2, width, half), bf16),
            dma((2, blocks, 2, 4)), dma((blocks, 4)), dma((2, nz, 4)), dma((2, 2, nz, 4)),
            dma((2, blocks, 4)), dma((3,)), dma((2,)), dma((2,)), dma((2, 2)), dma((2, 2)),
            dma((3,)), dma((4,)), dma((2,)),
        ],
        compiler_params=pltpu.CompilerParams(
            collective_id=0, has_side_effects=True, vmem_limit_bytes=VMEM_LIMIT),
    )(pair_density, energies[None, None, :], batch_live, coulomb_root[None, :])


def finish_kernel(
    factor, out_ref, at_ref, m_ref, w_ref, lead_ref, root_ref, polar_ref, screen_ref,
    round_ref, hold_ref, s_in, s_out,
):
    blocks, halves, _, half = out_ref.shape
    units = range(blocks * halves)
    takes = [
        pltpu.make_async_copy(
            out_ref.at[k // halves, k % halves], hold_ref.at[k], s_in.at[k]) for k in units
    ]
    puts = [
        pltpu.make_async_copy(
            hold_ref.at[k], polar_ref.at[:, k * half:(k + 1) * half], s_out.at[k]) for k in units
    ]
    for copy in takes:
        copy.start()

    def pass_on(some):
        for k in some:
            takes[k].wait()
            puts[k].start()
    packed = m_ref.shape[0]
    tile = 256
    for a in range(0, packed, tile):
        round_ref[a:a + tile, a:] = m_ref[a:a + tile, a:].astype(jnp.bfloat16)

    def apply(v):
        parts = []
        for a in range(0, packed, tile):
            e = a + tile
            part = jnp.dot(v[:, :e], round_ref[:e, a:e], preferred_element_type=jnp.float32)
            if e < packed:
                part += lax.dot_general(
                    v[:, e:], round_ref[a:e, e:], (((1,), (1,)), ((), ())),
                    preferred_element_type=jnp.float32)
            parts.append(part)
        return jnp.concatenate(parts, axis=1)

    cut = len(units) // 4
    pass_on(units[:cut])
    w = w_ref[...]
    q = (lead_ref[...].astype(jnp.float32) * root_ref[:, :CW]).T
    u = apply((q * w).astype(jnp.bfloat16))
    pass_on(units[cut:2 * cut])
    u += apply((u * (w * factor)).astype(jnp.bfloat16))
    pass_on(units[2 * cut:3 * cut])
    last = (q + factor * u).astype(jnp.bfloat16)
    screen_ref[...] = lax.dot_general(
        at_ref[...], last, (((1,), (1,)), ((), ())), preferred_element_type=jnp.float32)
    pass_on(units[3 * cut:])
    for copy in puts:
        copy.wait()


def finish(out, at, m, w, lead, coulomb_root):
    blocks, halves, width, half = out.shape
    packed = at.shape[1]
    vmem = pl.BlockSpec(memory_space=pltpu.VMEM)
    return pl.pallas_call(
        functools.partial(finish_kernel, 8.0 / G),
        out_shape=(
            jax.ShapeDtypeStruct((width, blocks * halves * half), jnp.bfloat16),
            jax.ShapeDtypeStruct((width, CW), jnp.float32),
        ),
        in_specs=[pl.BlockSpec(memory_space=pl.ANY)] + [vmem] * 5,
        out_specs=(pl.BlockSpec(memory_space=pl.ANY), vmem),
        scratch_shapes=[
            pltpu.VMEM((packed, packed), jnp.bfloat16),
            pltpu.VMEM((blocks * halves, width, half), jnp.bfloat16),
            pltpu.SemaphoreType.DMA((blocks * halves,)),
            pltpu.SemaphoreType.DMA((blocks * halves,)),
        ],
        compiler_params=pltpu.CompilerParams(vmem_limit_bytes=FINISH_LIMIT),
    )(out, at, m, w, lead, coulomb_root[None, :])


def body(pair_density, energies, batch_live, coulomb_root):
    blocks = lax.axis_size("blk")
    out, at, m, w, lead = stream(pair_density, energies, batch_live, coulomb_root, blocks)
    polarized, screened = finish(out, at, m, w, lead, coulomb_root)
    return (polarized[None], screened[None])


def solution(mesh):
    placed = (P("grp", "blk"), P("grp"), P(), P())
    aligned = (
        mesh.shape["grp"] == 4
        and mesh.shape["blk"] == 8
        and (G // mesh.shape["blk"]) % (LANES * 8) == 0
    )
    return jax.shard_map(
        body if aligned else plain_body,
        mesh=mesh,
        in_specs=placed,
        out_specs=(P("grp", "blk", None), P("grp", "blk", None)),
        check_vma=False,
    )
```

```python
import functools
import math

import jax
import jax.numpy as jnp
from jax import lax
from jax.experimental import pallas as pl
from jax.experimental.pallas import tpu as pltpu
from jax.sharding import PartitionSpec as P

G = 8192
CW = 128
DYSON = 2
LANES = 128
MESH = pl.DeviceIdType.MESH
VMEM_LIMIT = 30 * 1024 * 1024
FINISH_LIMIT = 10 * 1024 * 1024
OWN, XO, YO, YD, ZN, XN, YN, ZD, RD = range(9)
RELAY_Y = (2,)
EVENTS = (
    0, 1, 2, 3, 16, 17, 18, 19, 32, 33, 34, 35, 48, 49, 50, 51, 68, 69, 70, 71, 72, 73, 74,
    75, 76, 77, 78, 79, 84, 85, 86, 87, 88, 89, 90, 91, 92, 93, 94, 95, 100, 101, 102, 103,
    104, 105, 106, 107, 108, 109, 110, 111, 116, 117, 118, 120, 121, 122, 124, 125, 126, 135,
    139, 143,
)
PLANS = (
    (
        (
            0, 1, 68, 32, 2, 3, 16, 69, 18, 84, 19, 17, 50, 71, 34, 70, 48,
        ),
        (
            2, 1, 0, 4, 5, 3, 7, 12, 13, 6, 9, 14, 11, 15, 10, 8,
        ),
        (
            (), (101,), (76,), (), (85,), (51, 49), (35, 86, 87, 103), (92, 102, 33, 117, 78),
            (), (79,), (), (135, 108, 77, 94), (), (75, 95), (), (93, 73, 116), (), (100, 118,
            111, 91, 72), (), (89, 107), (110, 74), (124, 126), (105, 143), (109, 125, 139,
            121), (120, 104), (), (), (122, 106, 90, 88), (), (), (), (),
        ),
        (),
    ),
    (
        (
            0, 1, 68, 2, 3, 16, 17, 70, 74, 76, 72, 19, 84, 18, 78, 75, 69, 71, 73, 102,
        ),
        (
            0, 1, 4, 6, 3, 8, 2, 12, 14, 10, 9, 13, 7, 5, 11, 15,
        ),
        (
            (), (86,), (49, 100, 79, 116), (90, 118, 34), (77, 35), (33, 88), (117,), (104, 51,
            48), (), (32,), (126, 108, 92, 50, 94), (110,), (124, 91), (), (), (121, 101, 106,
            125, 120), (89, 107, 122, 85), (), (), (103, 87, 95), (), (93, 105), (), (135,),
            (111, 109), (), (), (139,), (143,), (), (), (),
        ),
        (),
    ),
)


def live_weights(all_energy, batch_live, slots, total_slots, group_ids, frequencies, norm_factor):
    positions = jnp.arange(total_slots, dtype=jnp.int32)
    owner_match = (positions // slots)[:, None] == group_ids[None, :]
    limits = jnp.sum(jnp.where(owner_match, batch_live[None, :], 0), axis=1)
    is_live = (positions % slots < limits).astype(jnp.float32)
    weight = (
        -2.0
        * all_energy[None, :]
        / (all_energy[None, :] * all_energy[None, :] + frequencies[:, None] * frequencies[:, None])
    )
    return weight * is_live[None, :] * norm_factor


def plain_body(pair_density, energies, batch_live, coulomb_root):
    slots = pair_density.shape[0]
    width_own = pair_density.shape[1]
    group_count = lax.axis_size("grp")
    block_count = lax.axis_size("blk")
    total_slots = slots * group_count
    group_index = lax.axis_index("grp")
    block_index = lax.axis_index("blk")
    norm_factor = 1.0 / math.sqrt(total_slots)
    own_root = lax.dynamic_slice_in_dim(coulomb_root, block_index * width_own, width_own)
    group_ids = jnp.arange(group_count, dtype=jnp.int32)
    row_density, all_energy = (
        lax.all_gather(pair_density, "grp", axis=0, tiled=True),
        lax.all_gather(energies.astype(jnp.bfloat16), "grp", axis=0, tiled=True).astype(
            energies.dtype
        ),
    )
    frequencies = 0.6 * jnp.arange(group_count, dtype=jnp.float32)
    weight = live_weights(
        all_energy, batch_live, slots, total_slots, group_ids, frequencies, norm_factor
    )
    scaled = (weight[:, :, None] * row_density.astype(jnp.float32)[None, :, :]).astype(jnp.bfloat16)
    sub_width = width_own // group_count
    my_slice = lax.dynamic_slice_in_dim(row_density, group_index * sub_width, sub_width, 1)
    root_table = jnp.reshape(coulomb_root, (block_count, group_count, sub_width))
    my_roots = jnp.reshape(
        lax.dynamic_index_in_dim(root_table, group_index, 1, keepdims=False), (-1,)
    )
    chi = jnp.einsum(
        "ftc,tk->fck",
        scaled,
        lax.all_gather(my_slice, "blk", axis=1, tiled=True),
        preferred_element_type=jnp.float32,
    )
    quarter = own_root[None, :, None] * chi * my_roots[None, None, :]
    received = lax.all_to_all(
        quarter.astype(jnp.bfloat16), "grp", split_axis=0, concat_axis=0, tiled=True
    )
    received = jnp.reshape(received, (group_count, width_own, block_count, sub_width))
    polarized = jnp.reshape(
        jnp.transpose(received, (1, 2, 0, 3)), (width_own, width_own * block_count)
    )
    lead_blocks = (CW + width_own - 1) // width_own
    lead = quarter[:, :, : lead_blocks * sub_width]
    lead_back = lax.all_to_all(
        lead.astype(jnp.bfloat16), "grp", split_axis=0, concat_axis=0, tiled=True
    ).astype(lead.dtype)
    lead_back = jnp.reshape(lead_back, (group_count, width_own, lead_blocks, sub_width))
    window = jnp.reshape(
        jnp.transpose(lead_back, (1, 2, 0, 3)), (width_own, lead_blocks * width_own)
    )[:, :CW]
    state = window
    for dyson_step in range(DYSON):
        rounded = state.astype(jnp.bfloat16)
        product = jnp.dot(
            polarized,
            lax.all_gather(rounded, "blk", axis=0, tiled=True),
            preferred_element_type=jnp.float32,
        )
        state = window + 8.0 / G * product
    return (polarized[None], state[None])


def far_plane(z, nz, k):
    edge = jnp.minimum(z, nz - 1 - z)
    low = k if k > 1 else jnp.where(edge == 0, k, 1 - k)
    return jnp.where(2 * z < nz, low, nz - 1 - low)


def stream_kernel(
    rows_ref, energy_ref, lives_ref, roots_ref,
    low_ref, high_ref, at_ref, m_ref, w_ref, lead_ref,
    p_ref, raw_ref, surplus_ref, spare_ref, energies_ref, column_ref, source_ref,
    pick_a, pick_b, pick_s, live_ref, root_ref,
    recv, s_x, s_y, s_z, s_pair, s_local, s_raw, r_raw, s_sur, r_sur, s_energy, r_energy,
):
    g, b = lax.axis_index("grp"), lax.axis_index("blk")
    x, c = g // 2, g % 2
    z, y = b // 2, b % 2
    nz = p_ref.shape[0] // 2
    slots, width = rows_ref.shape
    packed, half = p_ref.shape[2], p_ref.shape[3]
    share, core = packed // 2, packed // 4
    first = (packed - 2 * slots) // 2
    second = core - first
    edge = jnp.minimum(z, nz - 1 - z)
    to_x = ((1 - x) * 2 + c, b)
    to_y = (g, z * 2 + 1 - y)
    to_pair = (x * 2 + 1 - c, b)
    inward = jnp.where(2 * z < nz, z + 1, z - 1)
    outward = 2 * z - inward
    to_in = (g, inward * 2 + y)
    to_out = (g, outward * 2 + y)
    middle = edge == 1

    barrier = pltpu.get_barrier_semaphore()

    def greet(to):
        pl.semaphore_signal(barrier, inc=1, device_id=to, device_id_type=MESH)

    keep_rows = [
        pltpu.make_async_copy(
            rows_ref.at[:, h * half:(h + 1) * half],
            raw_ref.at[c, :, h * half:(h + 1) * half], s_local.at[h])
        for h in range(2)
    ]
    keep_energy = pltpu.make_async_copy(energy_ref.at[0], energies_ref.at[g], s_local.at[2])
    keep_live = pltpu.make_async_copy(lives_ref, live_ref, s_local.at[3])
    keep_root = pltpu.make_async_copy(roots_ref, root_ref, s_local.at[4])
    keep_live.start()
    for copy in keep_rows:
        copy.start()
    keep_energy.start()
    keep_root.start()
    for to in (to_x, to_y, to_pair, to_in):
        greet(to)
    pl.when(middle)(lambda: greet(to_out))
    pl.semaphore_wait(barrier, 4 + middle.astype(jnp.int32))

    def rows_pair(h, who):
        return pltpu.make_async_remote_copy(
            src_ref=rows_ref.at[:, h * half:(h + 1) * half],
            dst_ref=raw_ref.at[who, :, h * half:(h + 1) * half],
            send_sem=s_raw.at[h], recv_sem=r_raw.at[h], device_id=to_pair, device_id_type=MESH)

    def energy_to(way, to, who):
        return pltpu.make_async_remote_copy(
            src_ref=energies_ref.at[who] if way == 2 else energy_ref.at[0],
            dst_ref=energies_ref.at[who], send_sem=s_energy.at[way], recv_sem=r_energy.at[who],
            device_id=to, device_id_type=MESH)

    g_x, g_pair, g_far = (1 - x) * 2 + c, x * 2 + 1 - c, (1 - x) * 2 + 1 - c
    for h in range(2):
        rows_pair(h, c).start()
    energy_to(0, to_x, g).start()
    energy_to(1, to_pair, g).start()

    keep_live.wait()
    live0, live1 = live_ref[2 * x], live_ref[2 * x + 1]
    count = live0 + live1

    def one_hot(ref, source):
        at = lax.broadcasted_iota(jnp.int32, ref.shape, 1)
        ref[...] = (source == at).astype(jnp.float32).astype(jnp.bfloat16)

    def column_iota(size):
        return lax.broadcasted_iota(jnp.int32, (size, 1), 0)

    position = column_iota(pick_s.shape[0]) + (share + c * pick_s.shape[0])
    one_hot(pick_s, jnp.where(position < count, position - live0, -1))
    slot = column_iota(first) + c * first
    one_hot(pick_a, jnp.where(slot < live0, slot, slots + slot - live0))
    slot = column_iota(second) + (2 * first + c * second)
    one_hot(pick_b, jnp.where(
        slot < live0, slot,
        jnp.where(slot < count, slots + slot - live0, 2 * slots + slot - count)))

    def item(ox, ob, cc, kind, h):
        start = ox * share + cc * core + (first if kind else 0)
        size = second if kind else first
        return p_ref.at[ob, h, pl.ds(pl.multiple_of(start, 64), size)]

    def send(ox, ob, p, sem, to, cc=None, h=None):
        cc = c if cc is None else cc
        kind, h = (p // 2, p % 2) if h is None else (p, h)
        ref = item(ox, ob, cc, kind, h)
        return pltpu.make_async_remote_copy(
            src_ref=ref, dst_ref=ref, send_sem=sem, recv_sem=recv.at[ox, ob, cc, kind * 2 + h],
            device_id=to, device_id_type=MESH)

    def over_x(ox, ob, p):
        return send(ox, ob, p, s_x.at[ob, p], to_x)

    def over_y(ox, ob, p):
        return send(ox, ob, p, s_y.at[ox, ob // 2, p], to_y)

    def over_in(ox, ob, p):
        return send(ox, ob, p, s_z.at[0, ox, ob // 2, p], to_in)

    def over_out(ox, ob, p):
        return send(ox, ob, p, s_z.at[1, ox, ob // 2, p], to_out)

    def onward(ox, zz, ob, p):
        low = zz < z
        to = (g, jnp.where(low, z + 1, z - 1) * 2 + y)
        way = jnp.where(low == (2 * z < nz), 0, 1)
        return send(ox, ob, p, s_z.at[way, ox, zz, p], to)

    def over_pair(ox, ob, p):
        return send(ox, ob, p, s_pair.at[ox, ob, p], to_pair)

    def surplus_x(h):
        return pltpu.make_async_remote_copy(
            src_ref=spare_ref.at[h], dst_ref=surplus_ref.at[h, c], send_sem=s_sur.at[0, h],
            recv_sem=r_sur.at[h, c], device_id=to_x, device_id_type=MESH)

    def surplus_pair(h, who):
        return pltpu.make_async_remote_copy(
            src_ref=surplus_ref.at[h, who], dst_ref=surplus_ref.at[h, who],
            send_sem=s_sur.at[1, h], recv_sem=r_sur.at[h, who], device_id=to_pair,
            device_id_type=MESH)

    def dot(left, right):
        return jnp.dot(left, right, preferred_element_type=jnp.float32)

    def raw(who, h):
        return raw_ref[who, :, h * half:(h + 1) * half]

    def fill(kind, h, value):
        start = pl.multiple_of(x * share + c * core + (first if kind else 0), 64)
        value = value * root_ref[:, pl.ds(pl.multiple_of(b * width + h * half, half), half)]
        p_ref[b, h, pl.ds(start, second if kind else first)] = value.astype(jnp.bfloat16)

    for h in range(2):
        keep_rows[h].wait()
        rows_pair(h, 1 - c).wait_recv()
        spare_ref[h] = dot(pick_s[...], raw(1, h)).astype(jnp.bfloat16)
        surplus_x(h).start()
    keep_root.wait()
    for h in range(2):
        fill(0, h, dot(pick_a[:, :slots], raw(0, h)) + dot(pick_a[:, slots:], raw(1, h)))

    def prepare(h):
        surplus_x(h).wait_recv()
        surplus_pair(h, c).start()
        value = dot(pick_b[:, :slots], raw(0, h)) + dot(pick_b[:, slots:2 * slots], raw(1, h))
        surplus_pair(h, 1 - c).wait_recv()
        tail = pick_b.shape[1] - 2 * slots
        value += dot(pick_b[:, 2 * slots:2 * slots + tail // 2], surplus_ref[h, 0])
        fill(1, h, value + dot(pick_b[:, 2 * slots + tail // 2:], surplus_ref[h, 1]))

    def event(code):
        t, k, p = code // 16, code // 4 % 4, code % 4
        zz = far_plane(z, nz, k) if k else z
        ox = x if t in (OWN, YO, ZN, YN) else 1 - x
        ob = zz * 2 + (y if t in (OWN, XO, ZN, XN) else 1 - y)
        if t == OWN:
            if p >= 2:
                prepare(p % 2)
        else:
            send(ox, ob, p, s_pair.at[ox, ob, p], to_pair).wait_recv()
        return moves(t, k, p, zz, ox, ob, "start")

    def moves(t, k, p, zz, ox, ob, act):
        def do(make):
            getattr(make(), act)()

        if t in (OWN, ZN):
            if t == ZN:
                pl.when(middle)(lambda: do(lambda: onward(ox, zz, ob, p)))
            else:
                do(lambda: over_in(ox, ob, p))
                pl.when(middle)(lambda: do(lambda: over_out(ox, ob, p)))
            do(lambda: over_y(ox, ob, p))
            do(lambda: over_x(ox, ob, p))
        elif t == ZD:
            pl.when(middle)(lambda: do(lambda: onward(ox, zz, ob, p)))
        elif t == XO:
            do(lambda: over_y(ox, ob, p))
        elif t == YD and p < 3:
            do(lambda: over_in(ox, ob, p))
            pl.when(middle)(lambda: do(lambda: over_out(ox, ob, p)))
        elif t == XN and p == 3 and k in RELAY_Y:
            do(lambda: over_y(ox, ob, p))
        elif t == YN and p == 3 and k not in RELAY_Y:
            do(lambda: over_x(ox, ob, p))
        do(lambda: over_pair(ox, ob, p))

    def run(plans):
        for kind, codes in enumerate(plans):
            if codes:
                @pl.when(edge == kind)
                def _():
                    for code in codes:
                        event(code)

    def weights():
        energy_to(0, to_x, g_x).wait_recv()
        energy_to(2, to_pair, g_x).start()
        keep_energy.wait()
        energy_to(1, to_pair, g_pair).wait_recv()
        energy_to(2, to_pair, g_far).wait_recv()
        for k in range(4):
            column_ref[k * slots:(k + 1) * slots] = jnp.broadcast_to(
                energies_ref[k], (LANES, slots)).T
        row = lax.broadcasted_iota(jnp.int32, (1, packed), 1)
        upper = row >= share
        row = row - jnp.where(upper, share, 0)
        other = row >= core
        row = row - jnp.where(other, core, 0)
        late = row >= first
        row = row + jnp.where(
            late, 2 * first - first + jnp.where(other, second, 0), jnp.where(other, first, 0))
        a0, a1, a2, a3 = (live_ref[k] for k in range(4))
        n0 = jnp.where(upper, a2, a0)
        n1 = n0 + jnp.where(upper, a3, a1)
        base = jnp.where(upper, 2 * slots, 0)
        across = jnp.where(upper, slots - a0, 3 * slots - a2) + share
        source_ref[...] = jnp.where(
            row < n0, base + row,
            jnp.where(row < n1, base + slots + row - n0, across + row - n1))

        @pl.loop(0, packed // LANES)
        def _(k):
            part = pl.ds(pl.multiple_of(k * LANES, LANES), LANES)
            hit = source_ref[:, part] == lax.broadcasted_iota(
                jnp.int32, (4 * slots, LANES), 0)
            w_ref[:, part] = jnp.sum(
                jnp.where(hit, column_ref[...], 0.0), axis=0, keepdims=True)

        energy = w_ref[...]
        frequency = 0.6 * g.astype(jnp.float32)
        w_ref[...] = -2.0 * energy / (energy * energy + frequency * frequency) * (
            1.0 / math.sqrt(4 * slots))

    m_ref[...] = jnp.zeros_like(m_ref)
    leading = [plan[0] for plan in PLANS]
    early = [codes[:2] for codes in leading]
    run(early)
    weights()
    run([codes[2:] for codes in leading])

    def from_pair(ox, ob, kind, h):
        send(ox, ob, kind, s_pair.at[ox, ob, kind * 2 + h], to_pair, cc=1 - c, h=h).wait_recv()

    def ready(ob, h):
        for ox in range(2):
            for kind in range(2):
                from_pair(ox, ob, kind, h)

    for h in range(2):
        ready(b, h)
        for k in range(2):
            part = slice(k * half // 2, (k + 1) * half // 2)
            own = p_ref[b, h, :, part].astype(jnp.float32)
            rows = slice(h * half + part.start, h * half + part.stop)
            at_ref[rows] = (own.T * w_ref[...]).astype(jnp.bfloat16)

    units = 4 * nz

    @pl.loop(0, units)
    def _(step):
        def pick(table):
            value = table[0]
            for k in range(1, units):
                value = jnp.where(step == k, table[k], value)
            return value

        unit = jnp.where(edge == 0, pick(PLANS[0][1]), pick(PLANS[1][1]))
        k, other, h = unit // 4, unit // 2 % 2, unit % 2
        zz = z
        for j in range(1, nz):
            zz = jnp.where(k == j, far_plane(z, nz, j), zz)
        ob = zz * 2 + jnp.where(other == 1, 1 - y, y)

        def slot_events(which):
            for s in range(units):
                codes = [plan[2][2 * s + which] for plan in PLANS]
                if any(codes):
                    @pl.when(step == s)
                    def _():
                        run(codes)

        slot_events(0)

        @pl.when(unit >= 2)
        def _():
            ready(ob, h)

        for first_block, tiles in ((0, low_ref), (nz, high_ref)):
            @pl.when(ob // nz == first_block // nz)
            def _():
                tiles[ob - first_block, h] = dot(at_ref[...], p_ref[ob, h]).astype(jnp.bfloat16)

        slot_events(1)
        for a in range(0, packed, 256):
            m_ref[a:a + 256, a:] += lax.dot_general(
                p_ref[ob, h, a:a + 256], p_ref[ob, h, a:], (((1,), (1,)), ((), ())),
                preferred_element_type=jnp.float32)

    run([plan[3] for plan in PLANS])
    lead_ref[...] = p_ref[0, 0, :, :CW]

    energy_to(0, to_x, g).wait_send()
    energy_to(1, to_pair, g).wait_send()
    energy_to(2, to_pair, g_x).wait_send()
    for h in range(2):
        rows_pair(h, c).wait_send()
        surplus_x(h).wait_send()
        surplus_pair(h, c).wait_send()
    for code in EVENTS:
        t, k, p = code // 16, code // 4 % 4, code % 4
        zz = far_plane(z, nz, k) if k else z
        ox = x if t in (OWN, YO, ZN, YN) else 1 - x
        ob = zz * 2 + (y if t in (OWN, XO, ZN, XN) else 1 - y)
        moves(t, k, p, zz, ox, ob, "wait_send")


def stream(pair_density, energies, batch_live, coulomb_root, blocks):
    slots, width = pair_density.shape
    packed = slots * 5 // 2
    half = width // 2
    first = (packed - 2 * slots) // 2
    second = packed // 4 - first
    spare = (2 * slots - packed // 2) // 2
    nz = blocks // 2
    dma = pltpu.SemaphoreType.DMA
    vmem = pl.BlockSpec(memory_space=pltpu.VMEM)
    bf16, f32 = jnp.bfloat16, jnp.float32
    return pl.pallas_call(
        stream_kernel,
        out_shape=(
            pltpu.VMEM((nz, 2, width, half), bf16),
            pltpu.VMEM((nz, 2, width, half), bf16),
            pltpu.VMEM((width, packed), bf16),
            pltpu.VMEM((packed, packed), f32),
            pltpu.VMEM((1, packed), f32),
            pltpu.VMEM((packed, CW), bf16),
        ),
        in_specs=[pl.BlockSpec(memory_space=pltpu.HBM)] * 4,
        out_specs=(vmem,) * 6,
        scratch_shapes=[
            pltpu.VMEM((blocks, 2, packed, half), bf16),
            pltpu.VMEM((2, slots, width), bf16),
            pltpu.VMEM((2, 2, spare, half), bf16),
            pltpu.VMEM((2, spare, half), bf16),
            pltpu.VMEM((4, 1, slots), f32),
            pltpu.VMEM((4 * slots, LANES), f32),
            pltpu.VMEM((1, packed), jnp.int32),
            pltpu.VMEM((first, 2 * slots), bf16),
            pltpu.VMEM((second, 2 * slots + 2 * spare), bf16),
            pltpu.VMEM((spare, slots), bf16),
            pltpu.SMEM((4,), jnp.int32),
            pltpu.VMEM((1, coulomb_root.shape[0]), f32),
            dma((2, blocks, 2, 4)), dma((blocks, 4)), dma((2, nz, 4)), dma((2, 2, nz, 4)),
            dma((2, blocks, 4)), dma((5,)), dma((2,)), dma((2,)), dma((2, 2)), dma((2, 2)),
            dma((3,)), dma((4,)),
        ],
        compiler_params=pltpu.CompilerParams(
            collective_id=0, has_side_effects=True, vmem_limit_bytes=VMEM_LIMIT),
    )(*(
        pltpu.with_memory_space_constraint(value, pltpu.HBM)
        for value in (pair_density, energies[None, None, :], batch_live, coulomb_root[None, :])
    ))


def finish_kernel(
    factor, low_ref, high_ref, at_ref, m_ref, w_ref, lead_ref, polar_ref, screen_ref,
    round_ref, sems,
):
    count, halves, _, half = low_ref.shape
    tiles = [ref.at[k, h] for ref in (low_ref, high_ref) for k in range(count) for h in range(halves)]
    copies = [
        pltpu.make_async_copy(tile, polar_ref.at[:, k * half:(k + 1) * half], sems.at[k])
        for k, tile in enumerate(tiles)
    ]
    for copy in copies:
        copy.start()
    packed = m_ref.shape[0]
    tile = 256
    for a in range(0, packed, tile):
        round_ref[a:a + tile, a:] = m_ref[a:a + tile, a:].astype(jnp.bfloat16)

    def apply(v):
        parts = []
        for a in range(0, packed, tile):
            e = a + tile
            part = jnp.dot(v[:, :e], round_ref[:e, a:e], preferred_element_type=jnp.float32)
            if e < packed:
                part += lax.dot_general(
                    v[:, e:], round_ref[a:e, e:], (((1,), (1,)), ((), ())),
                    preferred_element_type=jnp.float32)
            parts.append(part)
        return jnp.concatenate(parts, axis=1)

    w = w_ref[...]
    q = lead_ref[...].astype(jnp.float32).T
    u = apply((q * w).astype(jnp.bfloat16))
    u += apply((u * (w * factor)).astype(jnp.bfloat16))
    last = (q + factor * u).astype(jnp.bfloat16)
    screen_ref[...] = lax.dot_general(
        at_ref[...], last, (((1,), (1,)), ((), ())), preferred_element_type=jnp.float32)
    for copy in copies:
        copy.wait()


def finish(low, high, at, m, w, lead):
    count, halves, width, half = low.shape
    units = 2 * count * halves
    packed = at.shape[1]
    vmem = pl.BlockSpec(memory_space=pltpu.VMEM)
    return pl.pallas_call(
        functools.partial(finish_kernel, 8.0 / G),
        out_shape=(
            jax.ShapeDtypeStruct((width, units * half), jnp.bfloat16),
            jax.ShapeDtypeStruct((width, CW), jnp.float32),
        ),
        in_specs=[vmem] * 6,
        out_specs=(pl.BlockSpec(memory_space=pl.ANY), vmem),
        scratch_shapes=[
            pltpu.VMEM((packed, packed), jnp.bfloat16),
            pltpu.SemaphoreType.DMA((units,)),
        ],
        compiler_params=pltpu.CompilerParams(vmem_limit_bytes=FINISH_LIMIT),
    )(*(
        pltpu.with_memory_space_constraint(value, pltpu.VMEM)
        for value in (low, high, at, m, w, lead)
    ))


def body(pair_density, energies, batch_live, coulomb_root):
    blocks = lax.axis_size("blk")
    streamed = stream(pair_density, energies, batch_live, coulomb_root, blocks)
    polarized, screened = finish(*streamed)
    return (polarized[None], screened[None])


def solution(mesh):
    placed = (P("grp", "blk"), P("grp"), P(), P())
    aligned = (
        mesh.shape["grp"] == 4
        and mesh.shape["blk"] == 8
        and (G // mesh.shape["blk"]) % (LANES * 8) == 0
    )
    return jax.shard_map(
        body if aligned else plain_body,
        mesh=mesh,
        in_specs=placed,
        out_specs=(P("grp", "blk", None), P("grp", "blk", None)),
        check_vma=False,
    )
```

```python
import functools
import math

import jax
import jax.numpy as jnp
from jax import lax
from jax.experimental import pallas as pl
from jax.experimental.pallas import tpu as pltpu
from jax.sharding import PartitionSpec as P

G = 8192
CW = 128
DYSON = 2
LANES = 128
MESH = pl.DeviceIdType.MESH
VMEM_LIMIT = 30 * 1024 * 1024
FINISH_LIMIT = 10 * 1024 * 1024
OWN, XO, YO, YD, ZN, XN, YN, ZD, RD = range(9)
RELAY_Y = (2,)
EVENTS = (
    0, 1, 2, 3, 16, 17, 18, 19, 32, 33, 34, 35, 48, 49, 50, 51, 68, 69, 70, 71, 72, 73, 74,
    75, 76, 77, 78, 79, 84, 85, 86, 87, 88, 89, 90, 91, 92, 93, 94, 95, 100, 101, 102, 103,
    104, 105, 106, 107, 108, 109, 110, 111, 116, 117, 118, 120, 121, 122, 124, 125, 126, 135,
    139, 143,
)
PLANS = (
    (
        (
            0, 1, 68, 32, 2, 3, 16, 69, 18, 84, 19, 17, 50, 71, 34, 70, 48,
        ),
        (
            2, 1, 0, 4, 5, 3, 7, 12, 13, 6, 9, 14, 11, 15, 10, 8,
        ),
        (
            (), (101,), (76,), (), (85,), (51, 49), (35, 86, 87, 103), (92, 102, 33, 117, 78),
            (), (79,), (), (135, 108, 77, 94), (), (75, 95), (), (93, 73, 116), (), (100, 118,
            111, 91, 72), (), (89, 107), (110, 74), (124, 126), (105, 143), (109, 125, 139,
            121), (120, 104), (), (), (122, 106, 90, 88), (), (), (), (),
        ),
        (),
    ),
    (
        (
            0, 1, 68, 2, 3, 16, 17, 70, 74, 76, 72, 19, 84, 18, 78, 75, 69, 71, 73, 102,
        ),
        (
            0, 1, 4, 6, 3, 8, 2, 12, 14, 10, 9, 13, 7, 5, 11, 15,
        ),
        (
            (), (86,), (49, 100, 79, 116), (90, 118, 34), (77, 35), (33, 88), (117,), (104, 51,
            48), (), (32,), (126, 108, 92, 50, 94), (110,), (124, 91), (), (), (121, 101, 106,
            125, 120), (89, 107, 122, 85), (), (), (103, 87, 95), (), (93, 105), (), (135,),
            (111, 109), (), (), (139,), (143,), (), (), (),
        ),
        (),
    ),
)


def live_weights(all_energy, batch_live, slots, total_slots, group_ids, frequencies, norm_factor):
    positions = jnp.arange(total_slots, dtype=jnp.int32)
    owner_match = (positions // slots)[:, None] == group_ids[None, :]
    limits = jnp.sum(jnp.where(owner_match, batch_live[None, :], 0), axis=1)
    is_live = (positions % slots < limits).astype(jnp.float32)
    weight = (
        -2.0
        * all_energy[None, :]
        / (all_energy[None, :] * all_energy[None, :] + frequencies[:, None] * frequencies[:, None])
    )
    return weight * is_live[None, :] * norm_factor


def plain_body(pair_density, energies, batch_live, coulomb_root):
    slots = pair_density.shape[0]
    width_own = pair_density.shape[1]
    group_count = lax.axis_size("grp")
    block_count = lax.axis_size("blk")
    total_slots = slots * group_count
    group_index = lax.axis_index("grp")
    block_index = lax.axis_index("blk")
    norm_factor = 1.0 / math.sqrt(total_slots)
    own_root = lax.dynamic_slice_in_dim(coulomb_root, block_index * width_own, width_own)
    group_ids = jnp.arange(group_count, dtype=jnp.int32)
    row_density, all_energy = (
        lax.all_gather(pair_density, "grp", axis=0, tiled=True),
        lax.all_gather(energies.astype(jnp.bfloat16), "grp", axis=0, tiled=True).astype(
            energies.dtype
        ),
    )
    frequencies = 0.6 * jnp.arange(group_count, dtype=jnp.float32)
    weight = live_weights(
        all_energy, batch_live, slots, total_slots, group_ids, frequencies, norm_factor
    )
    scaled = (weight[:, :, None] * row_density.astype(jnp.float32)[None, :, :]).astype(jnp.bfloat16)
    sub_width = width_own // group_count
    my_slice = lax.dynamic_slice_in_dim(row_density, group_index * sub_width, sub_width, 1)
    root_table = jnp.reshape(coulomb_root, (block_count, group_count, sub_width))
    my_roots = jnp.reshape(
        lax.dynamic_index_in_dim(root_table, group_index, 1, keepdims=False), (-1,)
    )
    chi = jnp.einsum(
        "ftc,tk->fck",
        scaled,
        lax.all_gather(my_slice, "blk", axis=1, tiled=True),
        preferred_element_type=jnp.float32,
    )
    quarter = own_root[None, :, None] * chi * my_roots[None, None, :]
    received = lax.all_to_all(
        quarter.astype(jnp.bfloat16), "grp", split_axis=0, concat_axis=0, tiled=True
    )
    received = jnp.reshape(received, (group_count, width_own, block_count, sub_width))
    polarized = jnp.reshape(
        jnp.transpose(received, (1, 2, 0, 3)), (width_own, width_own * block_count)
    )
    lead_blocks = (CW + width_own - 1) // width_own
    lead = quarter[:, :, : lead_blocks * sub_width]
    lead_back = lax.all_to_all(
        lead.astype(jnp.bfloat16), "grp", split_axis=0, concat_axis=0, tiled=True
    ).astype(lead.dtype)
    lead_back = jnp.reshape(lead_back, (group_count, width_own, lead_blocks, sub_width))
    window = jnp.reshape(
        jnp.transpose(lead_back, (1, 2, 0, 3)), (width_own, lead_blocks * width_own)
    )[:, :CW]
    state = window
    for dyson_step in range(DYSON):
        rounded = state.astype(jnp.bfloat16)
        product = jnp.dot(
            polarized,
            lax.all_gather(rounded, "blk", axis=0, tiled=True),
            preferred_element_type=jnp.float32,
        )
        state = window + 8.0 / G * product
    return (polarized[None], state[None])


def far_plane(z, nz, k):
    edge = jnp.minimum(z, nz - 1 - z)
    low = k if k > 1 else jnp.where(edge == 0, k, 1 - k)
    return jnp.where(2 * z < nz, low, nz - 1 - low)


def place_of(step, units, edge, z, y, nz):
    def pick(table):
        if isinstance(step, int):
            return table[step]
        value = table[0]
        for k in range(1, units):
            value = jnp.where(step == k, table[k], value)
        return value

    unit = jnp.where(edge == 0, pick(PLANS[0][1]), pick(PLANS[1][1]))
    k, other = unit // 4, unit // 2 % 2
    zz = z
    for j in range(1, nz):
        zz = jnp.where(k == j, far_plane(z, nz, j), zz)
    return zz * 2 + jnp.where(other == 1, 1 - y, y), unit % 2


def stream_kernel(
    rows_ref, energy_ref, lives_ref, roots_ref,
    tiles0_ref, tiles1_ref, tiles2_ref, tiles3_ref,
    at_ref, m_ref, w_ref, lead_ref, late_ref,
    p_ref, raw_ref, surplus_ref, spare_ref, energies_ref, column_ref, source_ref,
    pick_a, pick_b, pick_s, live_ref, root_ref,
    recv, s_x, s_y, s_z, s_pair, s_local, s_raw, r_raw, s_sur, r_sur, s_energy, r_energy, s_late,
):
    g, b = lax.axis_index("grp"), lax.axis_index("blk")
    x, c = g // 2, g % 2
    z, y = b // 2, b % 2
    nz = p_ref.shape[0] // 2
    slots, width = rows_ref.shape
    packed, half = p_ref.shape[2], p_ref.shape[3]
    share, core = packed // 2, packed // 4
    first = (packed - 2 * slots) // 2
    second = core - first
    edge = jnp.minimum(z, nz - 1 - z)
    to_x = ((1 - x) * 2 + c, b)
    to_y = (g, z * 2 + 1 - y)
    to_pair = (x * 2 + 1 - c, b)
    inward = jnp.where(2 * z < nz, z + 1, z - 1)
    outward = 2 * z - inward
    to_in = (g, inward * 2 + y)
    to_out = (g, outward * 2 + y)
    middle = edge == 1

    barrier = pltpu.get_barrier_semaphore()

    def greet(to):
        pl.semaphore_signal(barrier, inc=1, device_id=to, device_id_type=MESH)

    keep_rows = [
        pltpu.make_async_copy(
            rows_ref.at[:, h * half:(h + 1) * half],
            raw_ref.at[c, :, h * half:(h + 1) * half], s_local.at[h])
        for h in range(2)
    ]
    keep_energy = pltpu.make_async_copy(energy_ref.at[0], energies_ref.at[g], s_local.at[2])
    keep_live = pltpu.make_async_copy(lives_ref, live_ref, s_local.at[3])
    keep_root = pltpu.make_async_copy(roots_ref, root_ref, s_local.at[4])
    keep_live.start()
    for copy in keep_rows:
        copy.start()
    keep_energy.start()
    keep_root.start()
    for to in (to_x, to_y, to_pair, to_in):
        greet(to)
    pl.when(middle)(lambda: greet(to_out))

    def rows_pair(h, who):
        return pltpu.make_async_remote_copy(
            src_ref=rows_ref.at[:, h * half:(h + 1) * half],
            dst_ref=raw_ref.at[who, :, h * half:(h + 1) * half],
            send_sem=s_raw.at[h], recv_sem=r_raw.at[h], device_id=to_pair, device_id_type=MESH)

    def energy_to(way, to, who):
        return pltpu.make_async_remote_copy(
            src_ref=energies_ref.at[who] if way == 2 else energy_ref.at[0],
            dst_ref=energies_ref.at[who], send_sem=s_energy.at[way], recv_sem=r_energy.at[who],
            device_id=to, device_id_type=MESH)

    keep_live.wait()
    live0, live1 = live_ref[2 * x], live_ref[2 * x + 1]
    count = live0 + live1

    def one_hot(ref, source):
        at = lax.broadcasted_iota(jnp.int32, ref.shape, 1)
        ref[...] = (source == at).astype(jnp.float32).astype(jnp.bfloat16)

    def column_iota(size):
        return lax.broadcasted_iota(jnp.int32, (size, 1), 0)

    position = column_iota(pick_s.shape[0]) + (share + c * pick_s.shape[0])
    one_hot(pick_s, jnp.where(position < count, position - live0, -1))
    slot = column_iota(first) + c * first
    one_hot(pick_a, jnp.where(slot < live0, slot, slots + slot - live0))
    slot = column_iota(second) + (2 * first + c * second)
    one_hot(pick_b, jnp.where(
        slot < live0, slot,
        jnp.where(slot < count, slots + slot - live0, 2 * slots + slot - count)))

    m_ref[...] = jnp.zeros_like(m_ref)
    pl.semaphore_wait(barrier, 4 + middle.astype(jnp.int32))

    g_x, g_pair, g_far = (1 - x) * 2 + c, x * 2 + 1 - c, (1 - x) * 2 + 1 - c
    for h in range(2):
        rows_pair(h, c).start()
    energy_to(0, to_x, g).start()
    energy_to(1, to_pair, g).start()

    def item(ox, ob, cc, kind, h):
        start = ox * share + cc * core + (first if kind else 0)
        size = second if kind else first
        return p_ref.at[ob, h, pl.ds(pl.multiple_of(start, 64), size)]

    def send(ox, ob, p, sem, to, cc=None, h=None):
        cc = c if cc is None else cc
        kind, h = (p // 2, p % 2) if h is None else (p, h)
        ref = item(ox, ob, cc, kind, h)
        return pltpu.make_async_remote_copy(
            src_ref=ref, dst_ref=ref, send_sem=sem, recv_sem=recv.at[ox, ob, cc, kind * 2 + h],
            device_id=to, device_id_type=MESH)

    def over_x(ox, ob, p):
        return send(ox, ob, p, s_x.at[ob, p], to_x)

    def over_y(ox, ob, p):
        return send(ox, ob, p, s_y.at[ox, ob // 2, p], to_y)

    def over_in(ox, ob, p):
        return send(ox, ob, p, s_z.at[0, ox, ob // 2, p], to_in)

    def over_out(ox, ob, p):
        return send(ox, ob, p, s_z.at[1, ox, ob // 2, p], to_out)

    def onward(ox, zz, ob, p):
        low = zz < z
        to = (g, jnp.where(low, z + 1, z - 1) * 2 + y)
        way = jnp.where(low == (2 * z < nz), 0, 1)
        return send(ox, ob, p, s_z.at[way, ox, zz, p], to)

    def over_pair(ox, ob, p):
        return send(ox, ob, p, s_pair.at[ox, ob, p], to_pair)

    def surplus_x(h):
        return pltpu.make_async_remote_copy(
            src_ref=spare_ref.at[h], dst_ref=surplus_ref.at[h, c], send_sem=s_sur.at[0, h],
            recv_sem=r_sur.at[h, c], device_id=to_x, device_id_type=MESH)

    def surplus_pair(h, who):
        return pltpu.make_async_remote_copy(
            src_ref=surplus_ref.at[h, who], dst_ref=surplus_ref.at[h, who],
            send_sem=s_sur.at[1, h], recv_sem=r_sur.at[h, who], device_id=to_pair,
            device_id_type=MESH)

    def dot(left, right):
        return jnp.dot(left, right, preferred_element_type=jnp.float32)

    def raw(who, h):
        return raw_ref[who, :, h * half:(h + 1) * half]

    def fill(kind, h, value):
        start = pl.multiple_of(x * share + c * core + (first if kind else 0), 64)
        value = value * root_ref[:, pl.ds(pl.multiple_of(b * width + h * half, half), half)]
        p_ref[b, h, pl.ds(start, second if kind else first)] = value.astype(jnp.bfloat16)

    for h in range(2):
        keep_rows[h].wait()
        rows_pair(h, 1 - c).wait_recv()
        spare_ref[h] = dot(pick_s[...], raw(1, h)).astype(jnp.bfloat16)
        surplus_x(h).start()
    def prepare(h):
        surplus_x(h).wait_recv()
        surplus_pair(h, c).start()
        value = dot(pick_b[:, :slots], raw(0, h)) + dot(pick_b[:, slots:2 * slots], raw(1, h))
        surplus_pair(h, 1 - c).wait_recv()
        tail = pick_b.shape[1] - 2 * slots
        value += dot(pick_b[:, 2 * slots:2 * slots + tail // 2], surplus_ref[h, 0])
        fill(1, h, value + dot(pick_b[:, 2 * slots + tail // 2:], surplus_ref[h, 1]))

    def event(code):
        t, k, p = code // 16, code // 4 % 4, code % 4
        zz = far_plane(z, nz, k) if k else z
        ox = x if t in (OWN, YO, ZN, YN) else 1 - x
        ob = zz * 2 + (y if t in (OWN, XO, ZN, XN) else 1 - y)
        if t == OWN:
            if p >= 2:
                prepare(p % 2)
        else:
            send(ox, ob, p, s_pair.at[ox, ob, p], to_pair).wait_recv()
        return moves(t, k, p, zz, ox, ob, "start")

    def moves(t, k, p, zz, ox, ob, act):
        def do(make):
            getattr(make(), act)()

        if t in (OWN, ZN):
            if t == ZN:
                pl.when(middle)(lambda: do(lambda: onward(ox, zz, ob, p)))
            else:
                do(lambda: over_in(ox, ob, p))
                pl.when(middle)(lambda: do(lambda: over_out(ox, ob, p)))
            do(lambda: over_y(ox, ob, p))
            do(lambda: over_x(ox, ob, p))
        elif t == ZD:
            pl.when(middle)(lambda: do(lambda: onward(ox, zz, ob, p)))
        elif t == XO:
            do(lambda: over_y(ox, ob, p))
        elif t == YD and p < 3:
            do(lambda: over_in(ox, ob, p))
            pl.when(middle)(lambda: do(lambda: over_out(ox, ob, p)))
        elif t == XN and p == 3 and k in RELAY_Y:
            do(lambda: over_y(ox, ob, p))
        elif t == YN and p == 3 and k not in RELAY_Y:
            do(lambda: over_x(ox, ob, p))
        do(lambda: over_pair(ox, ob, p))

    def run(plans):
        for kind, codes in enumerate(plans):
            if codes:
                @pl.when(edge == kind)
                def _():
                    for code in codes:
                        event(code)

    def weights():
        energy_to(0, to_x, g_x).wait_recv()
        energy_to(2, to_pair, g_x).start()
        keep_energy.wait()
        energy_to(1, to_pair, g_pair).wait_recv()
        energy_to(2, to_pair, g_far).wait_recv()
        for k in range(4):
            column_ref[k * slots:(k + 1) * slots] = jnp.broadcast_to(
                energies_ref[k], (LANES, slots)).T
        row = lax.broadcasted_iota(jnp.int32, (1, packed), 1)
        upper = row >= share
        row = row - jnp.where(upper, share, 0)
        other = row >= core
        row = row - jnp.where(other, core, 0)
        late = row >= first
        row = row + jnp.where(
            late, 2 * first - first + jnp.where(other, second, 0), jnp.where(other, first, 0))
        a0, a1, a2, a3 = (live_ref[k] for k in range(4))
        n0 = jnp.where(upper, a2, a0)
        n1 = n0 + jnp.where(upper, a3, a1)
        base = jnp.where(upper, 2 * slots, 0)
        across = jnp.where(upper, slots - a0, 3 * slots - a2) + share
        source_ref[...] = jnp.where(
            row < n0, base + row,
            jnp.where(row < n1, base + slots + row - n0, across + row - n1))

        @pl.loop(0, packed // LANES)
        def _(k):
            part = pl.ds(pl.multiple_of(k * LANES, LANES), LANES)
            hit = source_ref[:, part] == lax.broadcasted_iota(
                jnp.int32, (4 * slots, LANES), 0)
            w_ref[:, part] = jnp.sum(
                jnp.where(hit, column_ref[...], 0.0), axis=0, keepdims=True)

        energy = w_ref[...]
        frequency = 0.6 * g.astype(jnp.float32)
        w_ref[...] = -2.0 * energy / (energy * energy + frequency * frequency) * (
            1.0 / math.sqrt(4 * slots))

    keep_root.wait()
    for h in range(2):
        fill(0, h, dot(pick_a[:, :slots], raw(0, h)) + dot(pick_a[:, slots:], raw(1, h)))
        event(h)
    weights()
    run([[code for code in plan[0] if code not in (0, 1)] for plan in PLANS])

    def from_pair(ox, ob, kind, h):
        send(ox, ob, kind, s_pair.at[ox, ob, kind * 2 + h], to_pair, cc=1 - c, h=h).wait_recv()

    def ready(ob, h):
        for ox in range(2):
            for kind in range(2):
                from_pair(ox, ob, kind, h)

    for h in range(2):
        ready(b, h)
        for k in range(2):
            part = slice(k * half // 2, (k + 1) * half // 2)
            own = p_ref[b, h, :, part].astype(jnp.float32)
            rows = slice(h * half + part.start, h * half + part.stop)
            at_ref[rows] = (own.T * w_ref[...]).astype(jnp.bfloat16)

    units = 4 * nz

    def slot_events(s):
        run([plan[2][s] for plan in PLANS])

    @pl.loop(0, units - 1)
    def _(step):
        ob, h = place_of(step, units, edge, z, y, nz)

        def events(which):
            for s in range(units - 1):
                if any(plan[2][2 * s + which] for plan in PLANS):
                    @pl.when(step == s)
                    def _():
                        slot_events(2 * s + which)

        events(0)

        @pl.when(ob != b)
        def _():
            ready(ob, h)

        for k, tiles in enumerate((tiles0_ref, tiles1_ref, tiles2_ref, tiles3_ref)):
            count = tiles.shape[0]

            @pl.when(ob // count == k)
            def _():
                tiles[ob - k * count, h] = dot(at_ref[...], p_ref[ob, h]).astype(jnp.bfloat16)

        events(1)

        @pl.when(step < units - 2)
        def _():
            for a in range(0, packed, 256):
                m_ref[a:a + 256, a:] += lax.dot_general(
                    p_ref[ob, h, a:a + 256], p_ref[ob, h, a:], (((1,), (1,)), ((), ())),
                    preferred_element_type=jnp.float32)

    def hand_on(k):
        ob, h = place_of(units - 2 + k, units, edge, z, y, nz)
        return pltpu.make_async_copy(p_ref.at[ob, h], late_ref.at[:, k * half:(k + 1) * half], s_late.at[k])

    hand_on(0).start()
    slot_events(2 * units - 2)
    slot_events(2 * units - 1)
    run([plan[3] for plan in PLANS])
    ob, h = place_of(units - 1, units, edge, z, y, nz)
    ready(ob, h)
    hand_on(1).start()
    lead_ref[...] = p_ref[0, 0, :, :CW]

    for k in range(2):
        hand_on(k).wait()
    energy_to(0, to_x, g).wait_send()
    energy_to(1, to_pair, g).wait_send()
    energy_to(2, to_pair, g_x).wait_send()
    for h in range(2):
        rows_pair(h, c).wait_send()
        surplus_x(h).wait_send()
        surplus_pair(h, c).wait_send()
    for code in EVENTS:
        t, k, p = code // 16, code // 4 % 4, code % 4
        zz = far_plane(z, nz, k) if k else z
        ox = x if t in (OWN, YO, ZN, YN) else 1 - x
        ob = zz * 2 + (y if t in (OWN, XO, ZN, XN) else 1 - y)
        moves(t, k, p, zz, ox, ob, "wait_send")


def stream(pair_density, energies, batch_live, coulomb_root, blocks):
    slots, width = pair_density.shape
    packed = slots * 5 // 2
    half = width // 2
    first = (packed - 2 * slots) // 2
    second = packed // 4 - first
    spare = (2 * slots - packed // 2) // 2
    nz = blocks // 2
    dma = pltpu.SemaphoreType.DMA
    vmem = pl.BlockSpec(memory_space=pltpu.VMEM)
    bf16, f32 = jnp.bfloat16, jnp.float32
    return pl.pallas_call(
        stream_kernel,
        out_shape=(
            *(pltpu.VMEM((nz // 2, 2, width, half), bf16),) * 4,
            pltpu.VMEM((width, packed), bf16),
            pltpu.VMEM((packed, packed), f32),
            pltpu.VMEM((1, packed), f32),
            pltpu.VMEM((packed, CW), bf16),
            pltpu.VMEM((packed, 2 * half), bf16),
        ),
        in_specs=[pl.BlockSpec(memory_space=pltpu.HBM)] * 4,
        out_specs=(vmem,) * 9,
        scratch_shapes=[
            pltpu.VMEM((blocks, 2, packed, half), bf16),
            pltpu.VMEM((2, slots, width), bf16),
            pltpu.VMEM((2, 2, spare, half), bf16),
            pltpu.VMEM((2, spare, half), bf16),
            pltpu.VMEM((4, 1, slots), f32),
            pltpu.VMEM((4 * slots, LANES), f32),
            pltpu.VMEM((1, packed), jnp.int32),
            pltpu.VMEM((first, 2 * slots), bf16),
            pltpu.VMEM((second, 2 * slots + 2 * spare), bf16),
            pltpu.VMEM((spare, slots), bf16),
            pltpu.SMEM((4,), jnp.int32),
            pltpu.VMEM((1, coulomb_root.shape[0]), f32),
            dma((2, blocks, 2, 4)), dma((blocks, 4)), dma((2, nz, 4)), dma((2, 2, nz, 4)),
            dma((2, blocks, 4)), dma((5,)), dma((2,)), dma((2,)), dma((2, 2)), dma((2, 2)),
            dma((3,)), dma((4,)), dma((2,)),
        ],
        compiler_params=pltpu.CompilerParams(
            collective_id=0, has_side_effects=True, vmem_limit_bytes=VMEM_LIMIT),
    )(*(
        pltpu.with_memory_space_constraint(value, pltpu.HBM)
        for value in (pair_density, energies[None, None, :], batch_live, coulomb_root[None, :])
    ))


def finish_kernel(
    factor, tiles0_ref, tiles1_ref, tiles2_ref, tiles3_ref,
    at_ref, m_ref, w_ref, lead_ref, late_ref, polar_ref, screen_ref,
    round_ref, last_ref, v_ref, u_ref, sems,
):
    b = lax.axis_index("blk")
    tiles = (tiles0_ref, tiles1_ref, tiles2_ref, tiles3_ref)
    count, halves, _, half = tiles[0].shape
    units = len(tiles) * count * halves
    nz = units // (2 * halves)
    z, y = b // 2, b % 2
    ob, h = place_of(units - 1, units, jnp.minimum(z, nz - 1 - z), z, y, nz)
    late = ob * halves + h

    def copy(k):
        return pltpu.make_async_copy(
            tiles[k // (halves * count)].at[k // halves % count, k % halves],
            polar_ref.at[:, k * half:(k + 1) * half], sems.at[k])

    for k in range(units):
        pl.when(late != k)(lambda k=k: copy(k).start())
    tile = 256

    @pl.loop(0, last_ref.shape[0] // tile)
    def _(k):
        rows = pl.ds(pl.multiple_of(k * tile, tile), tile)
        last_ref[rows] = jnp.dot(
            at_ref[rows], late_ref[:, half:], preferred_element_type=jnp.float32
        ).astype(jnp.bfloat16)

    start = pl.multiple_of(late * half, half)
    pltpu.make_async_copy(last_ref, polar_ref.at[:, pl.ds(start, half)], sems.at[late]).start()
    packed = m_ref.shape[0]

    for a in range(0, packed, tile):
        round_ref[a:a + tile, a:] = (m_ref[a:a + tile, a:] + lax.dot_general(
            late_ref[a:a + tile], late_ref[a:], (((1,), (1,)), ((), ())),
            preferred_element_type=jnp.float32)).astype(jnp.bfloat16)

    def apply(v):
        parts = []
        for a in range(0, packed, tile):
            e = a + tile
            part = jnp.dot(v[:, :e], round_ref[:e, a:e], preferred_element_type=jnp.float32)
            if e < packed:
                part += lax.dot_general(
                    v[:, e:], round_ref[a:e, e:], (((1,), (1,)), ((), ())),
                    preferred_element_type=jnp.float32)
            parts.append(part)
        return jnp.concatenate(parts, axis=1)

    w = w_ref[...]
    q = lead_ref[...].astype(jnp.float32).T
    v_ref[...] = (q * w).astype(jnp.bfloat16)
    u_ref[...] = jnp.zeros_like(u_ref)

    @pl.loop(0, DYSON)
    def _(_):
        u = apply(v_ref[...])
        u_ref[...] += u
        v_ref[...] = (u * (w_ref[...] * factor)).astype(jnp.bfloat16)

    u = u_ref[...]
    last = (q + factor * u).astype(jnp.bfloat16)
    screen_ref[...] = lax.dot_general(
        at_ref[...], last, (((1,), (1,)), ((), ())), preferred_element_type=jnp.float32)
    for k in range(units):
        copy(k).wait()


def finish(*streamed):
    tiles, at = streamed[:4], streamed[4]
    count, halves, width, half = tiles[0].shape
    units = len(tiles) * count * halves
    packed = at.shape[1]
    vmem = pl.BlockSpec(memory_space=pltpu.VMEM)
    return pl.pallas_call(
        functools.partial(finish_kernel, 8.0 / G),
        out_shape=(
            jax.ShapeDtypeStruct((width, units * half), jnp.bfloat16),
            jax.ShapeDtypeStruct((width, CW), jnp.float32),
        ),
        in_specs=[vmem] * 9,
        out_specs=(pl.BlockSpec(memory_space=pl.ANY), vmem),
        scratch_shapes=[
            pltpu.VMEM((packed, packed), jnp.bfloat16),
            pltpu.VMEM((width, half), jnp.bfloat16),
            pltpu.VMEM((CW, packed), jnp.bfloat16),
            pltpu.VMEM((CW, packed), jnp.float32),
            pltpu.SemaphoreType.DMA((units,)),
        ],
        compiler_params=pltpu.CompilerParams(vmem_limit_bytes=FINISH_LIMIT),
    )(*(
        pltpu.with_memory_space_constraint(value, pltpu.VMEM)
        for value in streamed
    ))


def body(pair_density, energies, batch_live, coulomb_root):
    blocks = lax.axis_size("blk")
    streamed = stream(pair_density, energies, batch_live, coulomb_root, blocks)
    polarized, screened = finish(*streamed)
    return (polarized[None], screened[None])


def solution(mesh):
    placed = (P("grp", "blk"), P("grp"), P(), P())
    aligned = (
        mesh.shape["grp"] == 4
        and mesh.shape["blk"] == 8
        and (G // mesh.shape["blk"]) % (LANES * 8) == 0
    )
    return jax.shard_map(
        body if aligned else plain_body,
        mesh=mesh,
        in_specs=placed,
        out_specs=(P("grp", "blk", None), P("grp", "blk", None)),
        check_vma=False,
    )
```

```python
import functools
import math

import jax
import jax.numpy as jnp
from jax import lax
from jax.experimental import pallas as pl
from jax.experimental.pallas import tpu as pltpu
from jax.sharding import PartitionSpec as P

G = 8192
CW = 128
DYSON = 2
LANES = 128
MESH = pl.DeviceIdType.MESH
VMEM_LIMIT = 30 * 1024 * 1024
FINISH_LIMIT = 10 * 1024 * 1024
OWN, XO, YO, YD, ZN, XN, YN, ZD, RD = range(9)
RELAY_Y = (2,)
EVENTS = (
    0, 1, 2, 3, 16, 17, 18, 19, 32, 33, 34, 35, 48, 49, 50, 51, 68, 69, 70, 71, 72, 73, 74,
    75, 76, 77, 78, 79, 84, 85, 86, 87, 88, 89, 90, 91, 92, 93, 94, 95, 100, 101, 102, 103,
    104, 105, 106, 107, 108, 109, 110, 111, 116, 117, 118, 120, 121, 122, 124, 125, 126, 135,
    139, 143,
)
PLANS = (
    (
        (
            0, 1, 68, 2, 3, 16, 69, 48, 17, 35, 18, 19, 34, 71, 84, 70,
        ),
        (
            0, 1, 2, 3, 4, 5, 12, 7, 13, 6, 9, 14, 11, 8, 15, 10,
        ),
        (
            (33,), (32,), (), (50, 78), (49,), (51, 86, 76, 101), (103, 87), (94,), (79, 77,
            102, 85), (), (), (92, 75, 116, 135, 117, 100, 110), (), (108, 95), (), (118, 73,
            93), (), (91, 74), (), (89, 72), (121, 126), (124, 107, 105, 111), (), (139, 90),
            (88, 109), (), (), (125, 143, 122, 106, 120, 104), (), (), (), (),
        ),
        (),
    ),
    (
        (
            0, 1, 68, 2, 3, 76, 70, 72, 17, 32, 100, 69, 33, 16, 18, 74, 19, 84, 71, 78, 77, 116,
        ),
        (
            0, 4, 1, 2, 6, 8, 3, 10, 5, 13, 14, 9, 12, 7, 11, 15,
        ),
        (
            (), (79, 86, 49), (92,), (102, 75), (48,), (104, 118, 85, 73, 34, 50, 35, 121, 88),
            (), (117, 90), (108,), (), (126, 124), (51, 101, 122), (120, 106), (87,), (), (93,),
            (95,), (125, 110), (94, 109), (91, 103), (89,), (), (), (135,), (107, 111), (105,),
            (), (139,), (143,), (), (), (),
        ),
        (),
    ),
)


def live_weights(all_energy, batch_live, slots, total_slots, group_ids, frequencies, norm_factor):
    positions = jnp.arange(total_slots, dtype=jnp.int32)
    owner_match = (positions // slots)[:, None] == group_ids[None, :]
    limits = jnp.sum(jnp.where(owner_match, batch_live[None, :], 0), axis=1)
    is_live = (positions % slots < limits).astype(jnp.float32)
    weight = (
        -2.0
        * all_energy[None, :]
        / (all_energy[None, :] * all_energy[None, :] + frequencies[:, None] * frequencies[:, None])
    )
    return weight * is_live[None, :] * norm_factor


def plain_body(pair_density, energies, batch_live, coulomb_root):
    slots = pair_density.shape[0]
    width_own = pair_density.shape[1]
    group_count = lax.axis_size("grp")
    block_count = lax.axis_size("blk")
    total_slots = slots * group_count
    group_index = lax.axis_index("grp")
    block_index = lax.axis_index("blk")
    norm_factor = 1.0 / math.sqrt(total_slots)
    own_root = lax.dynamic_slice_in_dim(coulomb_root, block_index * width_own, width_own)
    group_ids = jnp.arange(group_count, dtype=jnp.int32)
    row_density, all_energy = (
        lax.all_gather(pair_density, "grp", axis=0, tiled=True),
        lax.all_gather(energies.astype(jnp.bfloat16), "grp", axis=0, tiled=True).astype(
            energies.dtype
        ),
    )
    frequencies = 0.6 * jnp.arange(group_count, dtype=jnp.float32)
    weight = live_weights(
        all_energy, batch_live, slots, total_slots, group_ids, frequencies, norm_factor
    )
    scaled = (weight[:, :, None] * row_density.astype(jnp.float32)[None, :, :]).astype(jnp.bfloat16)
    sub_width = width_own // group_count
    my_slice = lax.dynamic_slice_in_dim(row_density, group_index * sub_width, sub_width, 1)
    root_table = jnp.reshape(coulomb_root, (block_count, group_count, sub_width))
    my_roots = jnp.reshape(
        lax.dynamic_index_in_dim(root_table, group_index, 1, keepdims=False), (-1,)
    )
    chi = jnp.einsum(
        "ftc,tk->fck",
        scaled,
        lax.all_gather(my_slice, "blk", axis=1, tiled=True),
        preferred_element_type=jnp.float32,
    )
    quarter = own_root[None, :, None] * chi * my_roots[None, None, :]
    received = lax.all_to_all(
        quarter.astype(jnp.bfloat16), "grp", split_axis=0, concat_axis=0, tiled=True
    )
    received = jnp.reshape(received, (group_count, width_own, block_count, sub_width))
    polarized = jnp.reshape(
        jnp.transpose(received, (1, 2, 0, 3)), (width_own, width_own * block_count)
    )
    lead_blocks = (CW + width_own - 1) // width_own
    lead = quarter[:, :, : lead_blocks * sub_width]
    lead_back = lax.all_to_all(
        lead.astype(jnp.bfloat16), "grp", split_axis=0, concat_axis=0, tiled=True
    ).astype(lead.dtype)
    lead_back = jnp.reshape(lead_back, (group_count, width_own, lead_blocks, sub_width))
    window = jnp.reshape(
        jnp.transpose(lead_back, (1, 2, 0, 3)), (width_own, lead_blocks * width_own)
    )[:, :CW]
    state = window
    for dyson_step in range(DYSON):
        rounded = state.astype(jnp.bfloat16)
        product = jnp.dot(
            polarized,
            lax.all_gather(rounded, "blk", axis=0, tiled=True),
            preferred_element_type=jnp.float32,
        )
        state = window + 8.0 / G * product
    return (polarized[None], state[None])


def far_plane(z, nz, k):
    edge = jnp.minimum(z, nz - 1 - z)
    low = k if k > 1 else jnp.where(edge == 0, k, 1 - k)
    return jnp.where(2 * z < nz, low, nz - 1 - low)


def place_of(step, units, edge, z, y, nz):
    def pick(table):
        if isinstance(step, int):
            return table[step]
        value = table[0]
        for k in range(1, units):
            value = jnp.where(step == k, table[k], value)
        return value

    unit = jnp.where(edge == 0, pick(PLANS[0][1]), pick(PLANS[1][1]))
    k, other = unit // 4, unit // 2 % 2
    zz = z
    for j in range(1, nz):
        zz = jnp.where(k == j, far_plane(z, nz, j), zz)
    return zz * 2 + jnp.where(other == 1, 1 - y, y), unit % 2


def stream_kernel(
    rows_ref, energy_ref, lives_ref, roots_ref,
    tiles0_ref, tiles1_ref, tiles2_ref, tiles3_ref,
    at_ref, m_ref, w_ref, lead_ref, late_ref,
    p_ref, raw_ref, surplus_ref, spare_ref, energies_ref, column_ref, source_ref,
    pick_a, pick_b, pick_s, live_ref, root_ref,
    recv, s_x, s_y, s_z, s_pair, s_local, s_raw, r_raw, s_sur, r_sur, s_energy, r_energy, s_late,
):
    g, b = lax.axis_index("grp"), lax.axis_index("blk")
    x, c = g // 2, g % 2
    z, y = b // 2, b % 2
    nz = p_ref.shape[0] // 2
    slots, width = rows_ref.shape
    packed, half = p_ref.shape[2], p_ref.shape[3]
    share, core = packed // 2, packed // 4
    first = (packed - 2 * slots) // 2
    second = core - first
    edge = jnp.minimum(z, nz - 1 - z)
    to_x = ((1 - x) * 2 + c, b)
    to_y = (g, z * 2 + 1 - y)
    to_pair = (x * 2 + 1 - c, b)
    inward = jnp.where(2 * z < nz, z + 1, z - 1)
    outward = 2 * z - inward
    to_in = (g, inward * 2 + y)
    to_out = (g, outward * 2 + y)
    middle = edge == 1

    barrier = pltpu.get_barrier_semaphore()

    def greet(to):
        pl.semaphore_signal(barrier, inc=1, device_id=to, device_id_type=MESH)

    keep_rows = [
        pltpu.make_async_copy(
            rows_ref.at[:, h * half:(h + 1) * half],
            raw_ref.at[c, :, h * half:(h + 1) * half], s_local.at[h])
        for h in range(2)
    ]
    keep_energy = pltpu.make_async_copy(energy_ref.at[0], energies_ref.at[g], s_local.at[2])
    keep_live = pltpu.make_async_copy(lives_ref, live_ref, s_local.at[3])
    keep_root = pltpu.make_async_copy(roots_ref, root_ref, s_local.at[4])
    keep_live.start()
    for copy in keep_rows:
        copy.start()
    keep_energy.start()
    keep_root.start()
    for to in (to_x, to_y, to_pair, to_in):
        greet(to)
    pl.when(middle)(lambda: greet(to_out))

    def rows_pair(h, who):
        return pltpu.make_async_remote_copy(
            src_ref=rows_ref.at[:, h * half:(h + 1) * half],
            dst_ref=raw_ref.at[who, :, h * half:(h + 1) * half],
            send_sem=s_raw.at[h], recv_sem=r_raw.at[h], device_id=to_pair, device_id_type=MESH)

    def energy_to(way, to, who):
        return pltpu.make_async_remote_copy(
            src_ref=energies_ref.at[who] if way == 2 else energy_ref.at[0],
            dst_ref=energies_ref.at[who], send_sem=s_energy.at[way], recv_sem=r_energy.at[who],
            device_id=to, device_id_type=MESH)

    keep_live.wait()
    live0, live1 = live_ref[2 * x], live_ref[2 * x + 1]
    count = live0 + live1

    def one_hot(ref, source):
        at = lax.broadcasted_iota(jnp.int32, ref.shape, 1)
        ref[...] = (source == at).astype(jnp.float32).astype(jnp.bfloat16)

    def column_iota(size):
        return lax.broadcasted_iota(jnp.int32, (size, 1), 0)

    position = column_iota(pick_s.shape[0]) + (share + c * pick_s.shape[0])
    one_hot(pick_s, jnp.where(position < count, position - live0, -1))
    slot = column_iota(first) + c * first
    one_hot(pick_a, jnp.where(slot < live0, slot, slots + slot - live0))
    slot = column_iota(second) + (2 * first + c * second)
    one_hot(pick_b, jnp.where(
        slot < live0, slot,
        jnp.where(slot < count, slots + slot - live0, 2 * slots + slot - count)))

    m_ref[...] = jnp.zeros_like(m_ref)
    pl.semaphore_wait(barrier, 4 + middle.astype(jnp.int32))

    g_x, g_pair, g_far = (1 - x) * 2 + c, x * 2 + 1 - c, (1 - x) * 2 + 1 - c
    for h in range(2):
        rows_pair(h, c).start()
    energy_to(0, to_x, g).start()
    energy_to(1, to_pair, g).start()

    def item(ox, ob, cc, kind, h):
        start = ox * share + cc * core + (first if kind else 0)
        size = second if kind else first
        return p_ref.at[ob, h, pl.ds(pl.multiple_of(start, 64), size)]

    def send(ox, ob, p, sem, to, cc=None, h=None):
        cc = c if cc is None else cc
        kind, h = (p // 2, p % 2) if h is None else (p, h)
        ref = item(ox, ob, cc, kind, h)
        return pltpu.make_async_remote_copy(
            src_ref=ref, dst_ref=ref, send_sem=sem, recv_sem=recv.at[ox, ob, cc, kind * 2 + h],
            device_id=to, device_id_type=MESH)

    def over_x(ox, ob, p):
        return send(ox, ob, p, s_x.at[ob, p], to_x)

    def over_y(ox, ob, p):
        return send(ox, ob, p, s_y.at[ox, ob // 2, p], to_y)

    def over_in(ox, ob, p):
        return send(ox, ob, p, s_z.at[0, ox, ob // 2, p], to_in)

    def over_out(ox, ob, p):
        return send(ox, ob, p, s_z.at[1, ox, ob // 2, p], to_out)

    def onward(ox, zz, ob, p):
        low = zz < z
        to = (g, jnp.where(low, z + 1, z - 1) * 2 + y)
        way = jnp.where(low == (2 * z < nz), 0, 1)
        return send(ox, ob, p, s_z.at[way, ox, zz, p], to)

    def over_pair(ox, ob, p):
        return send(ox, ob, p, s_pair.at[ox, ob, p], to_pair)

    def surplus_x(h):
        return pltpu.make_async_remote_copy(
            src_ref=spare_ref.at[h], dst_ref=surplus_ref.at[h, c], send_sem=s_sur.at[0, h],
            recv_sem=r_sur.at[h, c], device_id=to_x, device_id_type=MESH)

    def surplus_pair(h, who):
        return pltpu.make_async_remote_copy(
            src_ref=surplus_ref.at[h, who], dst_ref=surplus_ref.at[h, who],
            send_sem=s_sur.at[1, h], recv_sem=r_sur.at[h, who], device_id=to_pair,
            device_id_type=MESH)

    def dot(left, right):
        return jnp.dot(left, right, preferred_element_type=jnp.float32)

    def raw(who, h):
        return raw_ref[who, :, h * half:(h + 1) * half]

    def fill(kind, h, value):
        start = pl.multiple_of(x * share + c * core + (first if kind else 0), 64)
        value = value * root_ref[:, pl.ds(pl.multiple_of(b * width + h * half, half), half)]
        p_ref[b, h, pl.ds(start, second if kind else first)] = value.astype(jnp.bfloat16)

    def prepare(h):
        surplus_x(h).wait_recv()
        surplus_pair(h, c).start()
        value = dot(pick_b[:, :slots], raw(0, h)) + dot(pick_b[:, slots:2 * slots], raw(1, h))
        surplus_pair(h, 1 - c).wait_recv()
        tail = pick_b.shape[1] - 2 * slots
        value += dot(pick_b[:, 2 * slots:2 * slots + tail // 2], surplus_ref[h, 0])
        fill(1, h, value + dot(pick_b[:, 2 * slots + tail // 2:], surplus_ref[h, 1]))

    def event(code):
        t, k, p = code // 16, code // 4 % 4, code % 4
        zz = far_plane(z, nz, k) if k else z
        ox = x if t in (OWN, YO, ZN, YN) else 1 - x
        ob = zz * 2 + (y if t in (OWN, XO, ZN, XN) else 1 - y)
        if t == OWN:
            if p >= 2:
                prepare(p % 2)
        else:
            send(ox, ob, p, s_pair.at[ox, ob, p], to_pair).wait_recv()
        return moves(t, k, p, zz, ox, ob, "start")

    def moves(t, k, p, zz, ox, ob, act, across=True):
        def do(make):
            getattr(make(), act)()

        if t in (OWN, ZN):
            if t == ZN:
                pl.when(middle)(lambda: do(lambda: onward(ox, zz, ob, p)))
            else:
                do(lambda: over_in(ox, ob, p))
                pl.when(middle)(lambda: do(lambda: over_out(ox, ob, p)))
            do(lambda: over_y(ox, ob, p))
            if across:
                do(lambda: over_x(ox, ob, p))
        elif t == ZD:
            pl.when(middle)(lambda: do(lambda: onward(ox, zz, ob, p)))
        elif t == XO:
            do(lambda: over_y(ox, ob, p))
        elif t == YD and p < 3:
            do(lambda: over_in(ox, ob, p))
            pl.when(middle)(lambda: do(lambda: over_out(ox, ob, p)))
        elif t == XN and p == 3 and k in RELAY_Y:
            do(lambda: over_y(ox, ob, p))
        elif t == YN and p == 3 and k not in RELAY_Y:
            do(lambda: over_x(ox, ob, p))
        do(lambda: over_pair(ox, ob, p))

    def run(plans):
        for kind, codes in enumerate(plans):
            if codes:
                @pl.when(edge == kind)
                def _():
                    for code in codes:
                        event(code)

    def weights():
        energy_to(0, to_x, g_x).wait_recv()
        energy_to(2, to_pair, g_x).start()
        keep_energy.wait()
        energy_to(1, to_pair, g_pair).wait_recv()
        energy_to(2, to_pair, g_far).wait_recv()
        for k in range(4):
            column_ref[k * slots:(k + 1) * slots] = jnp.broadcast_to(
                energies_ref[k], (LANES, slots)).T
        row = lax.broadcasted_iota(jnp.int32, (1, packed), 1)
        upper = row >= share
        row = row - jnp.where(upper, share, 0)
        other = row >= core
        row = row - jnp.where(other, core, 0)
        late = row >= first
        row = row + jnp.where(
            late, 2 * first - first + jnp.where(other, second, 0), jnp.where(other, first, 0))
        a0, a1, a2, a3 = (live_ref[k] for k in range(4))
        n0 = jnp.where(upper, a2, a0)
        n1 = n0 + jnp.where(upper, a3, a1)
        base = jnp.where(upper, 2 * slots, 0)
        across = jnp.where(upper, slots - a0, 3 * slots - a2) + share
        source_ref[...] = jnp.where(
            row < n0, base + row,
            jnp.where(row < n1, base + slots + row - n0, across + row - n1))

        @pl.loop(0, packed // LANES)
        def _(k):
            part = pl.ds(pl.multiple_of(k * LANES, LANES), LANES)
            hit = source_ref[:, part] == lax.broadcasted_iota(
                jnp.int32, (4 * slots, LANES), 0)
            w_ref[:, part] = jnp.sum(
                jnp.where(hit, column_ref[...], 0.0), axis=0, keepdims=True)

        energy = w_ref[...]
        frequency = 0.6 * g.astype(jnp.float32)
        w_ref[...] = -2.0 * energy / (energy * energy + frequency * frequency) * (
            1.0 / math.sqrt(4 * slots))

    for h in range(2):
        keep_rows[h].wait()
        rows_pair(h, 1 - c).wait_recv()
        spare_ref[h] = dot(pick_s[...], raw(1, h)).astype(jnp.bfloat16)
        surplus_x(h).start()
        if h == 0:
            keep_root.wait()
        fill(0, h, dot(pick_a[:, :slots], raw(0, h)) + dot(pick_a[:, slots:], raw(1, h)))
        moves(OWN, 0, h, z, x, b, "start", across=False)
    for h in range(2):
        over_x(x, b, h).start()
    weights()
    run([[code for code in plan[0] if code not in (0, 1)] for plan in PLANS])

    def from_pair(ox, ob, kind, h):
        send(ox, ob, kind, s_pair.at[ox, ob, kind * 2 + h], to_pair, cc=1 - c, h=h).wait_recv()

    def ready(ob, h):
        for ox in range(2):
            for kind in range(2):
                from_pair(ox, ob, kind, h)

    for h in range(2):
        ready(b, h)
        for k in range(2):
            part = slice(k * half // 2, (k + 1) * half // 2)
            own = p_ref[b, h, :, part].astype(jnp.float32)
            rows = slice(h * half + part.start, h * half + part.stop)
            at_ref[rows] = (own.T * w_ref[...]).astype(jnp.bfloat16)

    units = 4 * nz

    def slot_events(s):
        run([plan[2][s] for plan in PLANS])

    @pl.loop(0, units - 1)
    def _(step):
        ob, h = place_of(step, units, edge, z, y, nz)

        def events(which):
            for s in range(units - 1):
                if any(plan[2][2 * s + which] for plan in PLANS):
                    @pl.when(step == s)
                    def _():
                        slot_events(2 * s + which)

        events(0)

        @pl.when(ob != b)
        def _():
            ready(ob, h)

        for k, tiles in enumerate((tiles0_ref, tiles1_ref, tiles2_ref, tiles3_ref)):
            count = tiles.shape[0]

            @pl.when(ob // count == k)
            def _():
                tiles[ob - k * count, h] = dot(at_ref[...], p_ref[ob, h]).astype(jnp.bfloat16)

        events(1)

        @pl.when(step < units - 2)
        def _():
            for a in range(0, packed, 256):
                m_ref[a:a + 256, a:] += lax.dot_general(
                    p_ref[ob, h, a:a + 256], p_ref[ob, h, a:], (((1,), (1,)), ((), ())),
                    preferred_element_type=jnp.float32)

    def hand_on(k):
        ob, h = place_of(units - 2 + k, units, edge, z, y, nz)
        return pltpu.make_async_copy(p_ref.at[ob, h], late_ref.at[:, k * half:(k + 1) * half], s_late.at[k])

    hand_on(0).start()
    slot_events(2 * units - 2)
    slot_events(2 * units - 1)
    run([plan[3] for plan in PLANS])
    ob, h = place_of(units - 1, units, edge, z, y, nz)

    def hand_item(ox, cc, kind):
        start = pl.multiple_of(ox * share + cc * core + (first if kind else 0), 64)
        rows = pl.ds(start, second if kind else first)
        sem = s_late.at[1 + ox * 4 + kind * 2 + jnp.where(cc == c, 0, 1)]
        return pltpu.make_async_copy(p_ref.at[ob, h, rows], late_ref.at[rows, half:], sem)

    def finish_sends(codes):
        for code in codes:
            t, k, p = code // 16, code // 4 % 4, code % 4
            zz = far_plane(z, nz, k) if k else z
            ox = x if t in (OWN, YO, ZN, YN) else 1 - x
            ob = zz * 2 + (y if t in (OWN, XO, ZN, XN) else 1 - y)
            moves(t, k, p, zz, ox, ob, "wait_send")

    quarters = [(ox, kind) for ox in range(2) for kind in range(2)]
    for ox, kind in quarters:
        hand_item(ox, c, kind).start()
    recent = {
        code for plan in PLANS for codes in (*plan[2][2 * units - 8:], plan[3]) for code in codes}
    lead_ref[...] = p_ref[0, 0, :, :CW]
    energy_to(0, to_x, g).wait_send()
    energy_to(1, to_pair, g).wait_send()
    energy_to(2, to_pair, g_x).wait_send()
    for k in range(2):
        rows_pair(k, c).wait_send()
        surplus_x(k).wait_send()
        surplus_pair(k, c).wait_send()
    hand_on(0).wait()
    finish_sends([code for code in EVENTS if code not in recent])
    for ox, kind in quarters:
        from_pair(ox, ob, kind, h)
        hand_item(ox, 1 - c, kind).start()
    finish_sends([code for code in EVENTS if code in recent])
    for ox, kind in quarters:
        hand_item(ox, c, kind).wait()
        hand_item(ox, 1 - c, kind).wait()


def stream(pair_density, energies, batch_live, coulomb_root, blocks):
    slots, width = pair_density.shape
    packed = slots * 5 // 2
    half = width // 2
    first = (packed - 2 * slots) // 2
    second = packed // 4 - first
    spare = (2 * slots - packed // 2) // 2
    nz = blocks // 2
    dma = pltpu.SemaphoreType.DMA
    vmem = pl.BlockSpec(memory_space=pltpu.VMEM)
    bf16, f32 = jnp.bfloat16, jnp.float32
    return pl.pallas_call(
        stream_kernel,
        out_shape=(
            *(pltpu.VMEM((nz // 2, 2, width, half), bf16),) * 4,
            pltpu.VMEM((width, packed), bf16),
            pltpu.VMEM((packed, packed), f32),
            pltpu.VMEM((1, packed), f32),
            pltpu.VMEM((packed, CW), bf16),
            pltpu.VMEM((packed, 2 * half), bf16),
        ),
        in_specs=[pl.BlockSpec(memory_space=pltpu.HBM)] * 4,
        out_specs=(vmem,) * 9,
        scratch_shapes=[
            pltpu.VMEM((blocks, 2, packed, half), bf16),
            pltpu.VMEM((2, slots, width), bf16),
            pltpu.VMEM((2, 2, spare, half), bf16),
            pltpu.VMEM((2, spare, half), bf16),
            pltpu.VMEM((4, 1, slots), f32),
            pltpu.VMEM((4 * slots, LANES), f32),
            pltpu.VMEM((1, packed), jnp.int32),
            pltpu.VMEM((first, 2 * slots), bf16),
            pltpu.VMEM((second, 2 * slots + 2 * spare), bf16),
            pltpu.VMEM((spare, slots), bf16),
            pltpu.SMEM((4,), jnp.int32),
            pltpu.VMEM((1, coulomb_root.shape[0]), f32),
            dma((2, blocks, 2, 4)), dma((blocks, 4)), dma((2, nz, 4)), dma((2, 2, nz, 4)),
            dma((2, blocks, 4)), dma((5,)), dma((2,)), dma((2,)), dma((2, 2)), dma((2, 2)),
            dma((3,)), dma((4,)), dma((9,)),
        ],
        compiler_params=pltpu.CompilerParams(
            collective_id=0, has_side_effects=True, vmem_limit_bytes=VMEM_LIMIT),
    )(*(
        pltpu.with_memory_space_constraint(value, pltpu.HBM)
        for value in (pair_density, energies[None, None, :], batch_live, coulomb_root[None, :])
    ))


def finish_kernel(
    factor, tiles0_ref, tiles1_ref, tiles2_ref, tiles3_ref,
    at_ref, m_ref, w_ref, lead_ref, late_ref, polar_ref, screen_ref,
    round_ref, last_ref, v_ref, u_ref, sems,
):
    b = lax.axis_index("blk")
    tiles = (tiles0_ref, tiles1_ref, tiles2_ref, tiles3_ref)
    count, halves, _, half = tiles[0].shape
    units = len(tiles) * count * halves
    nz = units // (2 * halves)
    z, y = b // 2, b % 2
    ob, h = place_of(units - 1, units, jnp.minimum(z, nz - 1 - z), z, y, nz)
    late = ob * halves + h

    def copy(k):
        return pltpu.make_async_copy(
            tiles[k // (halves * count)].at[k // halves % count, k % halves],
            polar_ref.at[:, k * half:(k + 1) * half], sems.at[k])

    for k in range(units):
        pl.when(late != k)(lambda k=k: copy(k).start())
    tile = 256

    @pl.loop(0, last_ref.shape[0] // tile)
    def _(k):
        rows = pl.ds(pl.multiple_of(k * tile, tile), tile)
        last_ref[rows] = jnp.dot(
            at_ref[rows], late_ref[:, half:], preferred_element_type=jnp.float32
        ).astype(jnp.bfloat16)

    start = pl.multiple_of(late * half, half)
    pltpu.make_async_copy(last_ref, polar_ref.at[:, pl.ds(start, half)], sems.at[late]).start()
    packed = m_ref.shape[0]

    for a in range(0, packed, tile):
        round_ref[a:a + tile, a:] = (m_ref[a:a + tile, a:] + lax.dot_general(
            late_ref[a:a + tile], late_ref[a:], (((1,), (1,)), ((), ())),
            preferred_element_type=jnp.float32)).astype(jnp.bfloat16)

    def apply(v):
        parts = []
        for a in range(0, packed, tile):
            e = a + tile
            part = jnp.dot(v[:, :e], round_ref[:e, a:e], preferred_element_type=jnp.float32)
            if e < packed:
                part += lax.dot_general(
                    v[:, e:], round_ref[a:e, e:], (((1,), (1,)), ((), ())),
                    preferred_element_type=jnp.float32)
            parts.append(part)
        return jnp.concatenate(parts, axis=1)

    w = w_ref[...]
    q = lead_ref[...].astype(jnp.float32).T
    v_ref[...] = (q * w).astype(jnp.bfloat16)
    u_ref[...] = jnp.zeros_like(u_ref)

    @pl.loop(0, DYSON)
    def _(_):
        u = apply(v_ref[...])
        u_ref[...] += u
        v_ref[...] = (u * (w_ref[...] * factor)).astype(jnp.bfloat16)

    u = u_ref[...]
    last = (q + factor * u).astype(jnp.bfloat16)
    screen_ref[...] = lax.dot_general(
        at_ref[...], last, (((1,), (1,)), ((), ())), preferred_element_type=jnp.float32)
    for k in range(units):
        copy(k).wait()


def finish(*streamed):
    tiles, at = streamed[:4], streamed[4]
    count, halves, width, half = tiles[0].shape
    units = len(tiles) * count * halves
    packed = at.shape[1]
    vmem = pl.BlockSpec(memory_space=pltpu.VMEM)
    return pl.pallas_call(
        functools.partial(finish_kernel, 8.0 / G),
        out_shape=(
            jax.ShapeDtypeStruct((width, units * half), jnp.bfloat16),
            jax.ShapeDtypeStruct((width, CW), jnp.float32),
        ),
        in_specs=[vmem] * 9,
        out_specs=(pl.BlockSpec(memory_space=pl.ANY), vmem),
        scratch_shapes=[
            pltpu.VMEM((packed, packed), jnp.bfloat16),
            pltpu.VMEM((width, half), jnp.bfloat16),
            pltpu.VMEM((CW, packed), jnp.bfloat16),
            pltpu.VMEM((CW, packed), jnp.float32),
            pltpu.SemaphoreType.DMA((units,)),
        ],
        compiler_params=pltpu.CompilerParams(vmem_limit_bytes=FINISH_LIMIT),
    )(*(
        pltpu.with_memory_space_constraint(value, pltpu.VMEM)
        for value in streamed
    ))


def body(pair_density, energies, batch_live, coulomb_root):
    blocks = lax.axis_size("blk")
    streamed = stream(pair_density, energies, batch_live, coulomb_root, blocks)
    polarized, screened = finish(*streamed)
    return (polarized[None], screened[None])


def solution(mesh):
    placed = (P("grp", "blk"), P("grp"), P(), P())
    aligned = (
        mesh.shape["grp"] == 4
        and mesh.shape["blk"] == 8
        and (G // mesh.shape["blk"]) % (LANES * 8) == 0
    )
    return jax.shard_map(
        body if aligned else plain_body,
        mesh=mesh,
        in_specs=placed,
        out_specs=(P("grp", "blk", None), P("grp", "blk", None)),
        check_vma=False,
    )
```

```python
import functools
import math

import jax
import jax.numpy as jnp
from jax import lax
from jax.experimental import pallas as pl
from jax.experimental.pallas import tpu as pltpu
from jax.sharding import PartitionSpec as P

G = 8192
CW = 128
DYSON = 2
LANES = 128
MESH = pl.DeviceIdType.MESH
VMEM_LIMIT = 30 * 1024 * 1024
FINISH_LIMIT = 10 * 1024 * 1024
OWN, XO, YO, YD, ZN, XN, YN, ZD, RD = range(9)
RELAY_Y = (2,)
EVENTS = (
    0, 1, 2, 3, 16, 17, 18, 19, 32, 33, 34, 35, 48, 49, 50, 51, 68, 69, 70, 71, 72, 73, 74,
    75, 76, 77, 78, 79, 84, 85, 86, 87, 88, 89, 90, 91, 92, 93, 94, 95, 100, 101, 102, 103,
    104, 105, 106, 107, 108, 109, 110, 111, 116, 117, 118, 120, 121, 122, 124, 125, 126, 135,
    139, 143,
)
PLANS = (
    (
        (
            0, 1, 68, 2, 3, 16, 69, 48, 17, 35, 18, 19, 34, 71, 84, 70,
        ),
        (
            0, 1, 2, 3, 4, 5, 12, 7, 13, 6, 9, 14, 11, 8, 15, 10,
        ),
        (
            (33,), (32,), (), (50, 78), (49,), (51, 86, 76, 101), (103, 87), (94,), (79, 77,
            102, 85), (), (), (92, 75, 116, 135, 117, 100, 110), (), (108, 95), (), (118, 73,
            93), (), (91, 74), (), (89, 72), (121, 126), (124, 107, 105, 111), (), (139, 90),
            (88, 109), (), (), (125, 143, 122, 106, 120, 104), (), (), (), (),
        ),
        (),
    ),
    (
        (
            0, 1, 68, 2, 3, 76, 70, 72, 17, 32, 100, 69, 33, 16, 18, 74, 19, 84, 71, 78, 77, 116,
        ),
        (
            0, 4, 1, 2, 6, 8, 3, 10, 5, 13, 14, 9, 12, 7, 11, 15,
        ),
        (
            (), (79, 86, 49), (92,), (102, 75), (48,), (104, 118, 85, 73, 34, 50, 35, 121, 88),
            (), (117, 90), (108,), (), (126, 124), (51, 101, 122), (120, 106), (87,), (), (93,),
            (95,), (125, 110), (94, 109), (91, 103), (89,), (), (), (135,), (107, 111), (105,),
            (), (139,), (143,), (), (), (),
        ),
        (),
    ),
)


def live_weights(all_energy, batch_live, slots, total_slots, group_ids, frequencies, norm_factor):
    positions = jnp.arange(total_slots, dtype=jnp.int32)
    owner_match = (positions // slots)[:, None] == group_ids[None, :]
    limits = jnp.sum(jnp.where(owner_match, batch_live[None, :], 0), axis=1)
    is_live = (positions % slots < limits).astype(jnp.float32)
    weight = (
        -2.0
        * all_energy[None, :]
        / (all_energy[None, :] * all_energy[None, :] + frequencies[:, None] * frequencies[:, None])
    )
    return weight * is_live[None, :] * norm_factor


def plain_body(pair_density, energies, batch_live, coulomb_root):
    slots = pair_density.shape[0]
    width_own = pair_density.shape[1]
    group_count = lax.axis_size("grp")
    block_count = lax.axis_size("blk")
    total_slots = slots * group_count
    group_index = lax.axis_index("grp")
    block_index = lax.axis_index("blk")
    norm_factor = 1.0 / math.sqrt(total_slots)
    own_root = lax.dynamic_slice_in_dim(coulomb_root, block_index * width_own, width_own)
    group_ids = jnp.arange(group_count, dtype=jnp.int32)
    row_density, all_energy = (
        lax.all_gather(pair_density, "grp", axis=0, tiled=True),
        lax.all_gather(energies.astype(jnp.bfloat16), "grp", axis=0, tiled=True).astype(
            energies.dtype
        ),
    )
    frequencies = 0.6 * jnp.arange(group_count, dtype=jnp.float32)
    weight = live_weights(
        all_energy, batch_live, slots, total_slots, group_ids, frequencies, norm_factor
    )
    scaled = (weight[:, :, None] * row_density.astype(jnp.float32)[None, :, :]).astype(jnp.bfloat16)
    sub_width = width_own // group_count
    my_slice = lax.dynamic_slice_in_dim(row_density, group_index * sub_width, sub_width, 1)
    root_table = jnp.reshape(coulomb_root, (block_count, group_count, sub_width))
    my_roots = jnp.reshape(
        lax.dynamic_index_in_dim(root_table, group_index, 1, keepdims=False), (-1,)
    )
    chi = jnp.einsum(
        "ftc,tk->fck",
        scaled,
        lax.all_gather(my_slice, "blk", axis=1, tiled=True),
        preferred_element_type=jnp.float32,
    )
    quarter = own_root[None, :, None] * chi * my_roots[None, None, :]
    received = lax.all_to_all(
        quarter.astype(jnp.bfloat16), "grp", split_axis=0, concat_axis=0, tiled=True
    )
    received = jnp.reshape(received, (group_count, width_own, block_count, sub_width))
    polarized = jnp.reshape(
        jnp.transpose(received, (1, 2, 0, 3)), (width_own, width_own * block_count)
    )
    lead_blocks = (CW + width_own - 1) // width_own
    lead = quarter[:, :, : lead_blocks * sub_width]
    lead_back = lax.all_to_all(
        lead.astype(jnp.bfloat16), "grp", split_axis=0, concat_axis=0, tiled=True
    ).astype(lead.dtype)
    lead_back = jnp.reshape(lead_back, (group_count, width_own, lead_blocks, sub_width))
    window = jnp.reshape(
        jnp.transpose(lead_back, (1, 2, 0, 3)), (width_own, lead_blocks * width_own)
    )[:, :CW]
    state = window
    for dyson_step in range(DYSON):
        rounded = state.astype(jnp.bfloat16)
        product = jnp.dot(
            polarized,
            lax.all_gather(rounded, "blk", axis=0, tiled=True),
            preferred_element_type=jnp.float32,
        )
        state = window + 8.0 / G * product
    return (polarized[None], state[None])


def far_plane(z, nz, k):
    edge = jnp.minimum(z, nz - 1 - z)
    low = k if k > 1 else jnp.where(edge == 0, k, 1 - k)
    return jnp.where(2 * z < nz, low, nz - 1 - low)


def place_of(step, units, edge, z, y, nz):
    def pick(table):
        if isinstance(step, int):
            return table[step]
        value = table[0]
        for k in range(1, units):
            value = jnp.where(step == k, table[k], value)
        return value

    unit = jnp.where(edge == 0, pick(PLANS[0][1]), pick(PLANS[1][1]))
    k, other = unit // 4, unit // 2 % 2
    zz = z
    for j in range(1, nz):
        zz = jnp.where(k == j, far_plane(z, nz, j), zz)
    return zz * 2 + jnp.where(other == 1, 1 - y, y), unit % 2


def stream_kernel(
    rows_ref, energy_ref, lives_ref, roots_ref,
    tiles0_ref, tiles1_ref, tiles2_ref, tiles3_ref,
    at_ref, m_ref, w_ref, lead_ref, late_ref,
    p_ref, raw_ref, surplus_ref, spare_ref, energies_ref, column_ref, source_ref,
    pick_a, pick_b, pick_s, live_ref, root_ref,
    recv, s_x, s_y, s_z, s_pair, s_local, s_raw, r_raw, s_sur, r_sur, s_energy, r_energy, s_late,
):
    g, b = lax.axis_index("grp"), lax.axis_index("blk")
    x, c = g // 2, g % 2
    z, y = b // 2, b % 2
    nz = p_ref.shape[0] // 2
    slots, width = rows_ref.shape
    packed, half = p_ref.shape[2], p_ref.shape[3]
    share, core = packed // 2, packed // 4
    first = (packed - 2 * slots) // 2
    second = core - first
    edge = jnp.minimum(z, nz - 1 - z)
    to_x = ((1 - x) * 2 + c, b)
    to_y = (g, z * 2 + 1 - y)
    to_pair = (x * 2 + 1 - c, b)
    inward = jnp.where(2 * z < nz, z + 1, z - 1)
    outward = 2 * z - inward
    to_in = (g, inward * 2 + y)
    to_out = (g, outward * 2 + y)
    middle = edge == 1

    barrier = pltpu.get_barrier_semaphore()

    def greet(to):
        pl.semaphore_signal(barrier, inc=1, device_id=to, device_id_type=MESH)

    keep_rows = [
        pltpu.make_async_copy(
            rows_ref.at[:, h * half:(h + 1) * half],
            raw_ref.at[c, :, h * half:(h + 1) * half], s_local.at[h])
        for h in range(2)
    ]
    keep_energy = pltpu.make_async_copy(energy_ref.at[0], energies_ref.at[g], s_local.at[2])
    keep_live = pltpu.make_async_copy(lives_ref, live_ref, s_local.at[3])
    keep_root = pltpu.make_async_copy(roots_ref, root_ref, s_local.at[4])
    keep_live.start()
    for copy in keep_rows:
        copy.start()
    keep_energy.start()
    keep_root.start()
    for to in (to_x, to_y, to_pair, to_in):
        greet(to)
    pl.when(middle)(lambda: greet(to_out))

    def rows_pair(h, tail, who):
        rows = pl.ds(2 * first if tail else 0, slots - 2 * first if tail else 2 * first)
        columns = slice(h * half, (h + 1) * half)
        return pltpu.make_async_remote_copy(
            src_ref=rows_ref.at[rows, columns], dst_ref=raw_ref.at[who, rows, columns],
            send_sem=s_raw.at[h, tail], recv_sem=r_raw.at[h, tail], device_id=to_pair,
            device_id_type=MESH)

    def energy_to(way, to, who):
        return pltpu.make_async_remote_copy(
            src_ref=energies_ref.at[who] if way == 2 else energy_ref.at[0],
            dst_ref=energies_ref.at[who], send_sem=s_energy.at[way], recv_sem=r_energy.at[who],
            device_id=to, device_id_type=MESH)

    keep_live.wait()
    live0, live1 = live_ref[2 * x], live_ref[2 * x + 1]
    count = live0 + live1

    def one_hot(ref, source):
        at = lax.broadcasted_iota(jnp.int32, ref.shape, 1)
        ref[...] = (source == at).astype(jnp.float32).astype(jnp.bfloat16)

    def column_iota(size):
        return lax.broadcasted_iota(jnp.int32, (size, 1), 0)

    position = column_iota(pick_s.shape[0]) + (share + c * pick_s.shape[0])
    one_hot(pick_s, jnp.where(position < count, position - live0, -1))
    slot = column_iota(first) + c * first
    one_hot(pick_a, jnp.where(slot < live0, slot, 2 * first + slot - live0))
    slot = column_iota(second) + (2 * first + c * second)
    one_hot(pick_b, jnp.where(
        slot < live0, slot,
        jnp.where(slot < count, slots + slot - live0, 2 * slots + slot - count)))

    m_ref[...] = jnp.zeros_like(m_ref)
    pl.semaphore_wait(barrier, 4 + middle.astype(jnp.int32))

    g_x, g_pair, g_far = (1 - x) * 2 + c, x * 2 + 1 - c, (1 - x) * 2 + 1 - c
    for h in range(2):
        for tail in range(2):
            rows_pair(h, tail, c).start()
    energy_to(0, to_x, g).start()
    energy_to(1, to_pair, g).start()

    def item(ox, ob, cc, kind, h):
        start = ox * share + cc * core + (first if kind else 0)
        size = second if kind else first
        return p_ref.at[ob, h, pl.ds(pl.multiple_of(start, 64), size)]

    def send(ox, ob, p, sem, to, cc=None, h=None):
        cc = c if cc is None else cc
        kind, h = (p // 2, p % 2) if h is None else (p, h)
        ref = item(ox, ob, cc, kind, h)
        return pltpu.make_async_remote_copy(
            src_ref=ref, dst_ref=ref, send_sem=sem, recv_sem=recv.at[ox, ob, cc, kind * 2 + h],
            device_id=to, device_id_type=MESH)

    def over_x(ox, ob, p):
        return send(ox, ob, p, s_x.at[ob, p], to_x)

    def over_y(ox, ob, p):
        return send(ox, ob, p, s_y.at[ox, ob // 2, p], to_y)

    def over_in(ox, ob, p):
        return send(ox, ob, p, s_z.at[0, ox, ob // 2, p], to_in)

    def over_out(ox, ob, p):
        return send(ox, ob, p, s_z.at[1, ox, ob // 2, p], to_out)

    def onward(ox, zz, ob, p):
        low = zz < z
        to = (g, jnp.where(low, z + 1, z - 1) * 2 + y)
        way = jnp.where(low == (2 * z < nz), 0, 1)
        return send(ox, ob, p, s_z.at[way, ox, zz, p], to)

    def over_pair(ox, ob, p):
        return send(ox, ob, p, s_pair.at[ox, ob, p], to_pair)

    def surplus_x(h):
        return pltpu.make_async_remote_copy(
            src_ref=spare_ref.at[h], dst_ref=surplus_ref.at[h, c], send_sem=s_sur.at[0, h],
            recv_sem=r_sur.at[h, c], device_id=to_x, device_id_type=MESH)

    def surplus_pair(h, who):
        return pltpu.make_async_remote_copy(
            src_ref=surplus_ref.at[h, who], dst_ref=surplus_ref.at[h, who],
            send_sem=s_sur.at[1, h], recv_sem=r_sur.at[h, who], device_id=to_pair,
            device_id_type=MESH)

    def dot(left, right):
        return jnp.dot(left, right, preferred_element_type=jnp.float32)

    def raw(who, h):
        return raw_ref[who, :, h * half:(h + 1) * half]

    def fill(kind, h, value):
        start = pl.multiple_of(x * share + c * core + (first if kind else 0), 64)
        value = value * root_ref[:, pl.ds(pl.multiple_of(b * width + h * half, half), half)]
        p_ref[b, h, pl.ds(start, second if kind else first)] = value.astype(jnp.bfloat16)

    def prepare(h):
        surplus_x(h).wait_recv()
        surplus_pair(h, c).start()
        value = dot(pick_b[:, :slots], raw(0, h)) + dot(pick_b[:, slots:2 * slots], raw(1, h))
        surplus_pair(h, 1 - c).wait_recv()
        tail = pick_b.shape[1] - 2 * slots
        value += dot(pick_b[:, 2 * slots:2 * slots + tail // 2], surplus_ref[h, 0])
        fill(1, h, value + dot(pick_b[:, 2 * slots + tail // 2:], surplus_ref[h, 1]))

    def event(code):
        t, k, p = code // 16, code // 4 % 4, code % 4
        zz = far_plane(z, nz, k) if k else z
        ox = x if t in (OWN, YO, ZN, YN) else 1 - x
        ob = zz * 2 + (y if t in (OWN, XO, ZN, XN) else 1 - y)
        if t == OWN:
            if p >= 2:
                prepare(p % 2)
        else:
            send(ox, ob, p, s_pair.at[ox, ob, p], to_pair).wait_recv()
        return moves(t, k, p, zz, ox, ob, "start")

    def moves(t, k, p, zz, ox, ob, act, across=True):
        def do(make):
            getattr(make(), act)()

        if t in (OWN, ZN):
            if t == ZN:
                pl.when(middle)(lambda: do(lambda: onward(ox, zz, ob, p)))
            else:
                do(lambda: over_in(ox, ob, p))
                pl.when(middle)(lambda: do(lambda: over_out(ox, ob, p)))
            do(lambda: over_y(ox, ob, p))
            if across:
                do(lambda: over_x(ox, ob, p))
        elif t == ZD:
            pl.when(middle)(lambda: do(lambda: onward(ox, zz, ob, p)))
        elif t == XO:
            do(lambda: over_y(ox, ob, p))
        elif t == YD and p < 3:
            do(lambda: over_in(ox, ob, p))
            pl.when(middle)(lambda: do(lambda: over_out(ox, ob, p)))
        elif t == XN and p == 3 and k in RELAY_Y:
            do(lambda: over_y(ox, ob, p))
        elif t == YN and p == 3 and k not in RELAY_Y:
            do(lambda: over_x(ox, ob, p))
        do(lambda: over_pair(ox, ob, p))

    def run(plans):
        for kind, codes in enumerate(plans):
            if codes:
                @pl.when(edge == kind)
                def _():
                    for code in codes:
                        event(code)

    def weights():
        energy_to(0, to_x, g_x).wait_recv()
        energy_to(2, to_pair, g_x).start()
        keep_energy.wait()
        energy_to(1, to_pair, g_pair).wait_recv()
        energy_to(2, to_pair, g_far).wait_recv()
        for k in range(4):
            column_ref[k * slots:(k + 1) * slots] = jnp.broadcast_to(
                energies_ref[k], (LANES, slots)).T
        row = lax.broadcasted_iota(jnp.int32, (1, packed), 1)
        upper = row >= share
        row = row - jnp.where(upper, share, 0)
        other = row >= core
        row = row - jnp.where(other, core, 0)
        late = row >= first
        row = row + jnp.where(
            late, 2 * first - first + jnp.where(other, second, 0), jnp.where(other, first, 0))
        a0, a1, a2, a3 = (live_ref[k] for k in range(4))
        n0 = jnp.where(upper, a2, a0)
        n1 = n0 + jnp.where(upper, a3, a1)
        base = jnp.where(upper, 2 * slots, 0)
        across = jnp.where(upper, slots - a0, 3 * slots - a2) + share
        source_ref[...] = jnp.where(
            row < n0, base + row,
            jnp.where(row < n1, base + slots + row - n0, across + row - n1))

        @pl.loop(0, packed // LANES)
        def _(k):
            part = pl.ds(pl.multiple_of(k * LANES, LANES), LANES)
            hit = source_ref[:, part] == lax.broadcasted_iota(
                jnp.int32, (4 * slots, LANES), 0)
            w_ref[:, part] = jnp.sum(
                jnp.where(hit, column_ref[...], 0.0), axis=0, keepdims=True)

        energy = w_ref[...]
        frequency = 0.6 * g.astype(jnp.float32)
        w_ref[...] = -2.0 * energy / (energy * energy + frequency * frequency) * (
            1.0 / math.sqrt(4 * slots))

    for h in range(2):
        keep_rows[h].wait()
        rows_pair(h, 0, 1 - c).wait_recv()
        if h == 0:
            keep_root.wait()
        head = 2 * first
        fill(0, h, dot(pick_a[:, :head], raw_ref[0, :head, h * half:(h + 1) * half]) + dot(
            pick_a[:, head:], raw_ref[1, :head, h * half:(h + 1) * half]))
        moves(OWN, 0, h, z, x, b, "start", across=False)
        rows_pair(h, 1, 1 - c).wait_recv()
        spare_ref[h] = dot(pick_s[...], raw(1, h)).astype(jnp.bfloat16)
        surplus_x(h).start()
    for h in range(2):
        over_x(x, b, h).start()
    weights()
    run([[code for code in plan[0] if code not in (0, 1)] for plan in PLANS])

    def from_pair(ox, ob, kind, h):
        send(ox, ob, kind, s_pair.at[ox, ob, kind * 2 + h], to_pair, cc=1 - c, h=h).wait_recv()

    def ready(ob, h):
        for ox in range(2):
            for kind in range(2):
                from_pair(ox, ob, kind, h)

    for h in range(2):
        ready(b, h)
        for k in range(2):
            part = slice(k * half // 2, (k + 1) * half // 2)
            own = p_ref[b, h, :, part].astype(jnp.float32)
            rows = slice(h * half + part.start, h * half + part.stop)
            at_ref[rows] = (own.T * w_ref[...]).astype(jnp.bfloat16)

    units = 4 * nz

    def slot_events(s):
        run([plan[2][s] for plan in PLANS])

    @pl.loop(0, units - 1)
    def _(step):
        ob, h = place_of(step, units, edge, z, y, nz)

        def events(which):
            for s in range(units - 1):
                if any(plan[2][2 * s + which] for plan in PLANS):
                    @pl.when(step == s)
                    def _():
                        slot_events(2 * s + which)

        events(0)

        @pl.when(ob != b)
        def _():
            ready(ob, h)

        for k, tiles in enumerate((tiles0_ref, tiles1_ref, tiles2_ref, tiles3_ref)):
            count = tiles.shape[0]

            @pl.when(ob // count == k)
            def _():
                tiles[ob - k * count, h] = dot(at_ref[...], p_ref[ob, h]).astype(jnp.bfloat16)

        events(1)

        @pl.when(step < units - 2)
        def _():
            for a in range(0, packed, 256):
                m_ref[a:a + 256, a:] += lax.dot_general(
                    p_ref[ob, h, a:a + 256], p_ref[ob, h, a:], (((1,), (1,)), ((), ())),
                    preferred_element_type=jnp.float32)

    def hand_on(k):
        ob, h = place_of(units - 2 + k, units, edge, z, y, nz)
        return pltpu.make_async_copy(p_ref.at[ob, h], late_ref.at[:, k * half:(k + 1) * half], s_late.at[k])

    hand_on(0).start()
    slot_events(2 * units - 2)
    slot_events(2 * units - 1)
    run([plan[3] for plan in PLANS])
    ob, h = place_of(units - 1, units, edge, z, y, nz)

    def hand_item(ox, cc, kind):
        start = pl.multiple_of(ox * share + cc * core + (first if kind else 0), 64)
        rows = pl.ds(start, second if kind else first)
        sem = s_late.at[1 + ox * 4 + kind * 2 + jnp.where(cc == c, 0, 1)]
        return pltpu.make_async_copy(p_ref.at[ob, h, rows], late_ref.at[rows, half:], sem)

    def finish_sends(codes):
        for code in codes:
            t, k, p = code // 16, code // 4 % 4, code % 4
            zz = far_plane(z, nz, k) if k else z
            ox = x if t in (OWN, YO, ZN, YN) else 1 - x
            ob = zz * 2 + (y if t in (OWN, XO, ZN, XN) else 1 - y)
            moves(t, k, p, zz, ox, ob, "wait_send")

    quarters = [(ox, kind) for ox in range(2) for kind in range(2)]
    for ox, kind in quarters:
        hand_item(ox, c, kind).start()
    recent = {
        code for plan in PLANS for codes in (*plan[2][2 * units - 8:], plan[3]) for code in codes}
    lead_ref[...] = p_ref[0, 0, :, :CW]
    energy_to(0, to_x, g).wait_send()
    energy_to(1, to_pair, g).wait_send()
    energy_to(2, to_pair, g_x).wait_send()
    for k in range(2):
        rows_pair(k, 0, c).wait_send()
        rows_pair(k, 1, c).wait_send()
        surplus_x(k).wait_send()
        surplus_pair(k, c).wait_send()
    hand_on(0).wait()
    finish_sends([code for code in EVENTS if code not in recent])
    for ox, kind in quarters:
        from_pair(ox, ob, kind, h)
        hand_item(ox, 1 - c, kind).start()
    finish_sends([code for code in EVENTS if code in recent])
    for ox, kind in quarters:
        hand_item(ox, c, kind).wait()
        hand_item(ox, 1 - c, kind).wait()


def stream(pair_density, energies, batch_live, coulomb_root, blocks):
    slots, width = pair_density.shape
    packed = slots * 5 // 2
    half = width // 2
    first = (packed - 2 * slots) // 2
    second = packed // 4 - first
    spare = (2 * slots - packed // 2) // 2
    nz = blocks // 2
    dma = pltpu.SemaphoreType.DMA
    vmem = pl.BlockSpec(memory_space=pltpu.VMEM)
    bf16, f32 = jnp.bfloat16, jnp.float32
    return pl.pallas_call(
        stream_kernel,
        out_shape=(
            *(pltpu.VMEM((nz // 2, 2, width, half), bf16),) * 4,
            pltpu.VMEM((width, packed), bf16),
            pltpu.VMEM((packed, packed), f32),
            pltpu.VMEM((1, packed), f32),
            pltpu.VMEM((packed, CW), bf16),
            pltpu.VMEM((packed, 2 * half), bf16),
        ),
        in_specs=[pl.BlockSpec(memory_space=pltpu.HBM)] * 4,
        out_specs=(vmem,) * 9,
        scratch_shapes=[
            pltpu.VMEM((blocks, 2, packed, half), bf16),
            pltpu.VMEM((2, slots, width), bf16),
            pltpu.VMEM((2, 2, spare, half), bf16),
            pltpu.VMEM((2, spare, half), bf16),
            pltpu.VMEM((4, 1, slots), f32),
            pltpu.VMEM((4 * slots, LANES), f32),
            pltpu.VMEM((1, packed), jnp.int32),
            pltpu.VMEM((first, 4 * first), bf16),
            pltpu.VMEM((second, 2 * slots + 2 * spare), bf16),
            pltpu.VMEM((spare, slots), bf16),
            pltpu.SMEM((4,), jnp.int32),
            pltpu.VMEM((1, coulomb_root.shape[0]), f32),
            dma((2, blocks, 2, 4)), dma((blocks, 4)), dma((2, nz, 4)), dma((2, 2, nz, 4)),
            dma((2, blocks, 4)), dma((5,)), dma((2, 2)), dma((2, 2)), dma((2, 2)), dma((2, 2)),
            dma((3,)), dma((4,)), dma((9,)),
        ],
        compiler_params=pltpu.CompilerParams(
            collective_id=0, has_side_effects=True, vmem_limit_bytes=VMEM_LIMIT),
    )(*(
        pltpu.with_memory_space_constraint(value, pltpu.HBM)
        for value in (pair_density, energies[None, None, :], batch_live, coulomb_root[None, :])
    ))


def finish_kernel(
    factor, tiles0_ref, tiles1_ref, tiles2_ref, tiles3_ref,
    at_ref, m_ref, w_ref, lead_ref, late_ref, polar_ref, screen_ref,
    round_ref, last_ref, v_ref, u_ref, sems,
):
    b = lax.axis_index("blk")
    tiles = (tiles0_ref, tiles1_ref, tiles2_ref, tiles3_ref)
    count, halves, _, half = tiles[0].shape
    units = len(tiles) * count * halves
    nz = units // (2 * halves)
    z, y = b // 2, b % 2
    ob, h = place_of(units - 1, units, jnp.minimum(z, nz - 1 - z), z, y, nz)
    late = ob * halves + h

    def copy(k):
        return pltpu.make_async_copy(
            tiles[k // (halves * count)].at[k // halves % count, k % halves],
            polar_ref.at[:, k * half:(k + 1) * half], sems.at[k])

    for k in range(units):
        pl.when(late != k)(lambda k=k: copy(k).start())
    tile = 256

    @pl.loop(0, last_ref.shape[0] // tile)
    def _(k):
        rows = pl.ds(pl.multiple_of(k * tile, tile), tile)
        last_ref[rows] = jnp.dot(
            at_ref[rows], late_ref[:, half:], preferred_element_type=jnp.float32
        ).astype(jnp.bfloat16)

    start = pl.multiple_of(late * half, half)
    pltpu.make_async_copy(last_ref, polar_ref.at[:, pl.ds(start, half)], sems.at[late]).start()
    packed = m_ref.shape[0]

    for a in range(0, packed, tile):
        round_ref[a:a + tile, a:] = (m_ref[a:a + tile, a:] + lax.dot_general(
            late_ref[a:a + tile], late_ref[a:], (((1,), (1,)), ((), ())),
            preferred_element_type=jnp.float32)).astype(jnp.bfloat16)

    def apply(v):
        parts = []
        for a in range(0, packed, tile):
            e = a + tile
            part = jnp.dot(v[:, :e], round_ref[:e, a:e], preferred_element_type=jnp.float32)
            if e < packed:
                part += lax.dot_general(
                    v[:, e:], round_ref[a:e, e:], (((1,), (1,)), ((), ())),
                    preferred_element_type=jnp.float32)
            parts.append(part)
        return jnp.concatenate(parts, axis=1)

    w = w_ref[...]
    q = lead_ref[...].astype(jnp.float32).T
    v_ref[...] = (q * w).astype(jnp.bfloat16)
    u_ref[...] = jnp.zeros_like(u_ref)

    @pl.loop(0, DYSON)
    def _(_):
        u = apply(v_ref[...])
        u_ref[...] += u
        v_ref[...] = (u * (w_ref[...] * factor)).astype(jnp.bfloat16)

    u = u_ref[...]
    last = (q + factor * u).astype(jnp.bfloat16)
    screen_ref[...] = lax.dot_general(
        at_ref[...], last, (((1,), (1,)), ((), ())), preferred_element_type=jnp.float32)
    for k in range(units):
        copy(k).wait()


def finish(*streamed):
    tiles, at = streamed[:4], streamed[4]
    count, halves, width, half = tiles[0].shape
    units = len(tiles) * count * halves
    packed = at.shape[1]
    vmem = pl.BlockSpec(memory_space=pltpu.VMEM)
    return pl.pallas_call(
        functools.partial(finish_kernel, 8.0 / G),
        out_shape=(
            jax.ShapeDtypeStruct((width, units * half), jnp.bfloat16),
            jax.ShapeDtypeStruct((width, CW), jnp.float32),
        ),
        in_specs=[vmem] * 9,
        out_specs=(pl.BlockSpec(memory_space=pl.ANY), vmem),
        scratch_shapes=[
            pltpu.VMEM((packed, packed), jnp.bfloat16),
            pltpu.VMEM((width, half), jnp.bfloat16),
            pltpu.VMEM((CW, packed), jnp.bfloat16),
            pltpu.VMEM((CW, packed), jnp.float32),
            pltpu.SemaphoreType.DMA((units,)),
        ],
        compiler_params=pltpu.CompilerParams(vmem_limit_bytes=FINISH_LIMIT),
    )(*(
        pltpu.with_memory_space_constraint(value, pltpu.VMEM)
        for value in streamed
    ))


def body(pair_density, energies, batch_live, coulomb_root):
    blocks = lax.axis_size("blk")
    streamed = stream(pair_density, energies, batch_live, coulomb_root, blocks)
    polarized, screened = finish(*streamed)
    return (polarized[None], screened[None])


def solution(mesh):
    placed = (P("grp", "blk"), P("grp"), P(), P())
    aligned = (
        mesh.shape["grp"] == 4
        and mesh.shape["blk"] == 8
        and (G // mesh.shape["blk"]) % (LANES * 8) == 0
    )
    return jax.shard_map(
        body if aligned else plain_body,
        mesh=mesh,
        in_specs=placed,
        out_specs=(P("grp", "blk", None), P("grp", "blk", None)),
        check_vma=False,
    )
```
